32 devices in a mesh: region: 16 (over z, y, core), tracer: 2 (over x).
Axes of the slice: x: 2, y: 2, z: 4, core: 2. Of those that a mesh axis runs over, the one named last changes fastest.
Arguments:
- tracers: float32 [256, 32, 6144], P('tracer', 'region'), may hold values from 0.2 to 1.5
- fluxes: float32 [2, 32, 6144], P(None, 'region', 'tracer'), may hold values from -0.4 to 0.4
- rate_coeff: float32 [1024], replicated, may hold values from 0.005 to 0.05
- first_reactant: int32 [1024], replicated, may hold values from 0 to 255
- second_reactant: int32 [1024], replicated, may hold values from 0 to 255
- product_species: int32 [1024], replicated, may hold values from 0 to 255
Outputs:
- tracers_out: float32 [256, 32, 6144], P('tracer', 'region')
The draws below stay inside these ranges and needn't reach their ends.
All inputs are finite; a program needn't handle non-finite values.
Results may differ from the reference program's by a relative error of at most 0.0001.
Values sent between devices are 32-bit elements; how exact they have to be, the bound alone decides.
A program may use at most 128 MiB of HBM per device.

```python
import math
import jax
import jax.numpy as jnp
from jax import lax

TRACERS = 256
REACTIONS = 1024
NY = 48
LEV = 128
CX = 2
ADV_STEPS = 2
SUBSTEPS = 4
NX = 32


def set_ends(values, rng, low, top_value):
    dims = values.shape
    place = [jax.random.randint(jax.random.fold_in(rng, axis), (), 0, dims[axis]) for axis in range(len(dims))]
    values = values.at[tuple(place)].set(low)
    longest = dims.index(max(dims))
    place[longest] = (place[longest] + 1) % dims[longest]
    return values.at[tuple(place)].set(top_value)


def steps_of(key, dims, split, least, largest):
    def one(dim, shards_of):
        steps = jax.random.uniform(jax.random.fold_in(jax.random.fold_in(key, 6), dim), (shards_of,), jnp.float32, least / len(split), largest / len(split))
        return jnp.repeat(jnp.exp(steps), dims[dim] // shards_of).reshape((-1,) + (1,) * (len(dims) - dim - 1))

    factor_of = one(*split[0])
    for cut in split[1:]:
        factor_of = factor_of * one(*cut)
    return factor_of


def setup_inputs(seed: int = 0) -> dict:
    key_list = jax.random.split(jax.random.key(seed), 7)
    tracers = jnp.clip(0.2 + 1.3 * jax.random.uniform(key_list[0], (TRACERS, NX, LEV * NY), jnp.float32) ** steps_of(key_list[0], (TRACERS, NX, LEV * NY), ((0, 2), (1, 16)), -0.2, 0.2), 0.2, 1.5)
    fluxes = jnp.clip(jax.random.uniform(key_list[1], (2, NX, LEV * NY), jnp.float32, -0.4, 0.4) * steps_of(key_list[1], (2, NX, LEV * NY), ((1, 16), (2, 2)), -0.4, 0.0), -0.4, 0.4)
    rate_coeff = jnp.clip(jnp.exp(jax.random.uniform(key_list[2], (REACTIONS,), jnp.float32, math.log(0.005), math.log(0.05))), 0.005, 0.05)
    first_reactant = set_ends(jax.random.randint(key_list[3], (REACTIONS,), 0, TRACERS), jax.random.fold_in(key_list[3], 1), 0, TRACERS - 1).astype(jnp.int32)
    second_reactant = set_ends(jax.random.randint(key_list[4], (REACTIONS,), 0, TRACERS), jax.random.fold_in(key_list[4], 1), 0, TRACERS - 1).astype(jnp.int32)
    product_species = set_ends(jax.random.randint(key_list[5], (REACTIONS,), 0, TRACERS), jax.random.fold_in(key_list[5], 1), 0, TRACERS - 1).astype(jnp.int32)
    return {"tracers": tracers, "fluxes": fluxes, "rate_coeff": rate_coeff, "first_reactant": first_reactant, "second_reactant": second_reactant, "product_species": product_species}


def advect(padded, courant, margin, wind_margin, row_len):
    length = padded.shape[1]
    offset = wind_margin - margin
    east_flow = courant[0, offset + 1: offset + length]
    flux_x = jnp.maximum(east_flow, 0.0) * padded[:, :-1] + jnp.minimum(east_flow, 0.0) * padded[:, 1:]
    central = padded[:, 1:-1]
    north_flow = courant[1, offset + 1: offset + length - 1]
    south_cell = jnp.roll(central, 1, axis=2)
    y_index = jnp.arange(central.shape[2], dtype=jnp.int32) % row_len
    flux_y = jnp.where(y_index == 0, 0.0, jnp.maximum(north_flow, 0.0) * south_cell + jnp.minimum(north_flow, 0.0) * central)
    return central + flux_x[:, :-1] - flux_x[:, 1:] + flux_y - jnp.roll(flux_y, -1, axis=2)


def tables(first_reactant, second_reactant, product_species, count):
    species = jnp.arange(count, dtype=jnp.int32)
    pick_first = (first_reactant[:, None] == species[None, :]).astype(jnp.float32)
    pick_second = (second_reactant[:, None] == species[None, :]).astype(jnp.float32)
    made = (product_species[:, None] == species[None, :]).astype(jnp.float32)
    change_table = jnp.transpose(made - pick_first - pick_second)
    return pick_first, pick_second, change_table


def chemistry_steps(amounts, rate_coeff, pick_first, pick_second, change_table):
    for repeat in range(SUBSTEPS):
        first = jnp.dot(pick_first, amounts, precision=lax.Precision.HIGHEST)
        second = jnp.dot(pick_second, amounts, precision=lax.Precision.HIGHEST)
        velocity = rate_coeff[:, None] * first * second
        amounts = amounts + jnp.dot(change_table, velocity, precision=lax.Precision.HIGHEST)
    return amounts


def reference(tracers, fluxes, rate_coeff, first_reactant, second_reactant, product_species):
    courant = jnp.concatenate([fluxes[:, -ADV_STEPS:], fluxes, fluxes[:, :ADV_STEPS]], axis=1)
    tracer_now = tracers
    for repeat in range(ADV_STEPS):
        padded = jnp.concatenate([tracer_now[:, -1:], tracer_now, tracer_now[:, :1]], axis=1)
        tracer_now = advect(padded, courant, 1, ADV_STEPS, NY)
    pick_first, pick_second, change_table = tables(first_reactant, second_reactant, product_species, TRACERS)
    block_size = CX * LEV * NY
    by_block = jnp.transpose(tracer_now.reshape(TRACERS, -1, block_size), (1, 0, 2))

    def chemistry(portion):
        return chemistry_steps(portion, rate_coeff, pick_first, pick_second, change_table)

    reacted = lax.map(chemistry, by_block)
    return jnp.transpose(reacted, (1, 0, 2)).reshape(tracer_now.shape)
```

```python
import functools

import jax
import jax.numpy as jnp
from jax import lax
from jax.experimental import pallas as pl
from jax.experimental.pallas import tpu as pltpu
from jax.sharding import PartitionSpec as P

NY = 48
SUBSTEPS = 4
LANES = 128
BLOCKS = 3
ROWS = 2 * BLOCKS
GROUP = BLOCKS * LANES


def ring(axis, by):
    length = lax.axis_size(axis)
    return [(i, (i + by) % length) for i in range(length)]


def swap_pairs(rows, even):
    return jnp.where(even, pltpu.roll(rows, 7, 0), pltpu.roll(rows, 1, 0))


def south_north(rows, lane):
    south = pltpu.roll(rows, 1, 1)
    south = jnp.where(lane == 0, pltpu.roll(south, 2, 0), south)
    north = pltpu.roll(rows, LANES - 1, 1)
    north = jnp.where(lane == LANES - 1, pltpu.roll(north, 6, 0), north)
    return south, north


def advect_rows(own, west, east, coef, even, lane):
    edge = jnp.where(even, east, west)
    outer = jnp.where(even, west, east)

    def step(center, inner, out, base):
        south, north = south_north(center, lane)
        return (
            coef[base] * center
            + coef[base + 1] * inner
            + coef[base + 2] * out
            + coef[base + 3] * south
            + coef[base + 4] * north
        )

    own_swap = swap_pairs(own, even)
    new_own = step(own, own_swap, swap_pairs(edge, even), 0)
    new_edge = step(edge, own_swap, swap_pairs(outer, even), 5)
    return step(new_own, swap_pairs(new_own, even), swap_pairs(new_edge, even), 0)


def react_kernel(parts, groups, count, *refs):
    first_ref, second_ref, rate_ref, table_ref, coef_ref = refs[:5]
    own_refs = refs[5 : 5 + parts]
    west_refs = refs[5 + parts : 5 + 2 * parts]
    east_refs = refs[5 + 2 * parts : 5 + 3 * parts]
    out_refs = refs[5 + 3 * parts : 5 + 4 * parts]
    c_ref, w_ref = refs[5 + 4 * parts :]
    reactions = first_ref.shape[0]
    species = parts * count
    quad = 4 * groups * ROWS
    row = lax.broadcasted_iota(jnp.int32, (8, LANES), 0)
    lane = lax.broadcasted_iota(jnp.int32, (8, LANES), 1)
    even = row % 2 == 0

    def rows_of(ref, base, off):
        if off + 8 <= quad:
            return ref[pl.ds(base + off, 8), :]
        return pltpu.roll(ref[pl.ds(base + quad - 8, 8), :], 6, 0)

    for part in range(parts):
        for group in range(groups):
            coef = [coef_ref[k, group] for k in range(10)]

            def advect_four(i, carry, part=part, group=group, coef=coef):
                base = pl.multiple_of(i * quad, 8)
                for j in range(4):
                    off = (j * groups + group) * ROWS
                    values = [
                        rows_of(ref[part], base, off) for ref in (own_refs, west_refs, east_refs)
                    ]
                    start = (part * count + i * 4 + j) * (groups * 8 + 1) + group * 8
                    c_ref[pl.ds(start, 8), :] = advect_rows(*values, coef, even, lane)
                return carry

            lax.fori_loop(0, count // 4, advect_four, 0)

    height = groups * 8
    pitch = height + 1
    unroll = 16

    def react(step, carry):
        def velocities(i, carry):
            for j in range(unroll):
                r = i * unroll + j
                first = first_ref[r]
                second = second_ref[r]
                for g in range(groups):
                    w_ref[pl.ds(r * pitch + g * 8, 8), :] = (
                        rate_ref[r]
                        * c_ref[pl.ds(first + g * 8, 8), :]
                        * c_ref[pl.ds(second + g * 8, 8), :]
                    )
            return carry

        lax.fori_loop(0, reactions // unroll, velocities, 0)

        for group in range(groups):
            for k in range(ROWS):
                at = group * 8 + k
                w = w_ref[pl.ds(at, reactions, stride=pitch), :]
                high = w.astype(jnp.bfloat16)
                low = (w - high.astype(jnp.float32)).astype(jnp.bfloat16)
                change = jnp.dot(
                    table_ref[...],
                    jnp.concatenate([high, low], axis=1),
                    preferred_element_type=jnp.float32,
                )
                where = pl.ds(at, species, stride=pitch)
                c_ref[where, :] = c_ref[where, :] + (change[:, :LANES] + change[:, LANES:])
        return carry

    lax.fori_loop(0, SUBSTEPS, react, 0)

    for part in range(parts):

        def put_four(i, carry, part=part):
            base = pl.multiple_of(i * quad, 8)
            for j in range(4):
                for group in range(groups):
                    start = (part * count + i * 4 + j) * (groups * 8 + 1) + group * 8
                    out_refs[part][pl.ds(base + (j * groups + group) * ROWS, ROWS), :] = c_ref[
                        pl.ds(start, ROWS), :
                    ]
            return carry

        lax.fori_loop(0, count // 4, put_four, 0)


def react_chunk(first, second, rate, table, coef, own, west, east, count):
    parts = len(own)
    groups = coef.shape[1]
    reactions = first.shape[0]
    species = parts * count
    smem = pl.BlockSpec(memory_space=pltpu.SMEM)
    vmem = pl.BlockSpec(memory_space=pltpu.VMEM)
    cells = species * groups * GROUP * 2
    return pl.pallas_call(
        functools.partial(react_kernel, parts, groups, count),
        out_shape=[jax.ShapeDtypeStruct(own[0].shape, jnp.float32)] * parts,
        in_specs=[smem] * 3 + [vmem] * (2 + 3 * parts),
        out_specs=[vmem] * parts,
        scratch_shapes=[
            pltpu.VMEM((species * (groups * 8 + 1) + 7, LANES), jnp.float32),
            pltpu.VMEM((reactions * (groups * 8 + 1) + 7, LANES), jnp.float32),
        ],
        cost_estimate=pl.CostEstimate(
            flops=cells * reactions * 2 * 2 * SUBSTEPS, bytes_accessed=cells * 4 * 4, transcendentals=0
        ),
        compiler_params=pltpu.CompilerParams(vmem_limit_bytes=40 * 1024 * 1024),
        name=f"react_{groups}",
    )(first, second, rate, table, coef, *own, *west, *east)


def coefficients(fluxes, from_west, from_east):
    u, v = fluxes[0], fluxes[1]
    uw, vw = from_west[0], from_west[1]
    ue, ve = from_east[0], from_east[1]
    y = jnp.arange(u.shape[1], dtype=jnp.int32) % NY
    bottom, top = y == 0, y == NY - 1

    def up(values):
        return jnp.maximum(values, 0.0)

    def down(values):
        return jnp.minimum(values, 0.0)

    def rows(west_face, east_face, face_in, face_out, v_here):
        above = jnp.roll(v_here, -1, axis=1)
        center = (
            1.0
            + down(west_face)
            - up(east_face)
            + jnp.where(bottom, 0.0, down(v_here))
            - jnp.where(top, 0.0, up(above))
        )
        south = jnp.where(bottom, 0.0, up(v_here))
        north = jnp.where(top, 0.0, -down(above))
        return [center, face_in, face_out, south, north]

    u0, u1, u2, u3, um = u[0], u[1], ue[0], ue[1], uw[1]
    own = rows(
        jnp.stack([u0, u1]),
        jnp.stack([u1, u2]),
        jnp.stack([-down(u1), up(u1)]),
        jnp.stack([up(u0), -down(u2)]),
        v,
    )
    edge = rows(
        jnp.stack([u2, um]),
        jnp.stack([u3, u0]),
        jnp.stack([up(u2), -down(u0)]),
        jnp.stack([-down(u3), up(um)]),
        jnp.stack([ve[0], vw[1]]),
    )
    coef = jnp.stack(own + edge)
    count = coef.shape[0]
    coef = coef.reshape(count, 2, -1, BLOCKS, LANES).transpose(0, 2, 3, 1, 4)
    coef = coef.reshape(count, -1, ROWS, LANES)
    return jnp.pad(coef, ((0, 0), (0, 0), (0, 8 - ROWS), (0, 0)))


def chunk_sizes(total):
    if total >= 8:
        return [2, total - 4, 2]
    return [1] * total


def body(tracers, fluxes, rate_coeff, first_reactant, second_reactant, product_species):
    parts = lax.axis_size("tracer")
    me = lax.axis_index("tracer")
    count, columns, length = tracers.shape
    blocks = length // LANES
    own_blocks = blocks // parts
    species = parts * count
    natural = tracers.reshape(count, columns, blocks, LANES).transpose(0, 2, 1, 3)

    from_west = lax.ppermute(fluxes, "region", ring("region", 1))
    from_east = lax.ppermute(fluxes, "region", ring("region", -1))

    chunks, at = [], 0
    for size in chunk_sizes(own_blocks // BLOCKS):
        chunks.append((at, size))
        at += size

    def piece(source, owner, start, size):
        taken = lax.dynamic_slice_in_dim(
            source, owner * own_blocks + start * BLOCKS, size * BLOCKS, axis=1
        )
        return taken.reshape(count * size * ROWS, LANES)

    owns, wests, easts = [], [], []
    for start, size in chunks:
        pieces = [piece(natural, (me + shift) % parts, start, size) for shift in range(parts)]
        if owns:
            pieces[1:], _ = lax.optimization_barrier((pieces[1:], owns[-1][1:]))
            pieces[0], _ = lax.optimization_barrier((pieces[0], (wests[0], easts[0])))
        own = pieces[:1]
        for shift in range(1, parts):
            own.append(lax.ppermute(pieces[shift], "tracer", ring("tracer", shift)))
        owns.append(own)
        wests.append([lax.ppermute(values, "region", ring("region", 1)) for values in own])
        easts.append([lax.ppermute(values, "region", ring("region", -1)) for values in own])

    coef = coefficients(fluxes, from_west, from_east)
    def place(index):
        return (me - index // count) % parts * count + index % count

    order = jnp.arange(species, dtype=jnp.int32)[:, None]
    first, second, product = (
        place(index) for index in (first_reactant, second_reactant, product_species)
    )
    table = (
        (product[None, :] == order).astype(jnp.float32)
        - (first[None, :] == order).astype(jnp.float32)
        - (second[None, :] == order).astype(jnp.float32)
    ).astype(jnp.bfloat16)

    by_shift = [[] for _ in range(parts)]
    for (start, size), own, west, east in zip(chunks, owns, wests, easts):
        reacted = react_chunk(
            first * (size * 8 + 1),
            second * (size * 8 + 1),
            rate_coeff,
            table,
            coef[:, start : start + size],
            own,
            west,
            east,
            count,
        )
        for shift in range(parts):
            values = reacted[shift]
            if shift:
                values = lax.ppermute(values, "tracer", ring("tracer", -shift))
            by_shift[shift].append(values.reshape(count, size * BLOCKS, columns, LANES))
    pieces = []
    for owner in range(parts):
        shift = (owner - me) % parts
        for at in range(len(chunks)):
            picked = by_shift[0][at]
            for other in range(1, parts):
                picked = jnp.where(shift == other, by_shift[other][at], picked)
            pieces.append(picked)
    out = jnp.concatenate(pieces, axis=1)
    return out.transpose(0, 2, 1, 3).reshape(tracers.shape)


def solution(mesh):
    in_specs = (P("tracer", "region", None), P(None, "region", "tracer"), P(), P(), P(), P())
    out_specs = P("tracer", "region", None)
    return jax.shard_map(body, mesh=mesh, in_specs=in_specs, out_specs=out_specs, check_vma=False)
```

```python
import functools

import jax
import jax.numpy as jnp
from jax import lax
from jax.experimental import pallas as pl
from jax.experimental.pallas import tpu as pltpu
from jax.sharding import PartitionSpec as P

NY = 48
SUBSTEPS = 4
LANES = 128
BLOCKS = 3
COLUMNS = 2
ROWS = COLUMNS * BLOCKS
GROUP = BLOCKS * LANES
PITCH = 9
MESH = pl.DeviceIdType.MESH


def south_of(values, lane):
    shifted = []
    for t in range(BLOCKS):
        source = values[t] if t == 0 else jnp.where(lane == LANES - 1, values[t - 1], values[t])
        shifted.append(pltpu.roll(source, 1, 1))
    return shifted


def north_of(values, lane):
    shifted = []
    for t in range(BLOCKS):
        last = t == BLOCKS - 1
        source = values[t] if last else jnp.where(lane == 0, values[t + 1], values[t])
        shifted.append(pltpu.roll(source, LANES - 1, 1))
    return shifted


def up(values):
    return jnp.maximum(values, 0.0)


def down(values):
    return jnp.minimum(values, 0.0)


def write_coefficients(groups, coef_ref, own_ref, west_ref, east_ref):
    lane = lax.broadcasted_iota(jnp.int32, (groups, LANES), 1)

    def read(ref, axis, column):
        rows = ref.reshape(2 * groups * ROWS, LANES)
        return [
            rows[pl.ds(axis * groups * ROWS + t * COLUMNS + column, groups, stride=ROWS), :]
            for t in range(BLOCKS)
        ]

    sources = ((west_ref, 1), (own_ref, 0), (own_ref, 1), (east_ref, 0), (east_ref, 1))
    u = [read(ref, 0, column) for ref, column in sources]
    for at in range(4):
        v = read(sources[at][0], 1, sources[at][1])
        above = north_of(v, lane)
        for t in range(BLOCKS):
            y = (lane + t * LANES) % NY
            bottom, top = y == 0, y == NY - 1
            west_face, east_face = u[at][t], u[at + 1][t]
            center = (
                1.0
                + down(west_face)
                - up(east_face)
                + jnp.where(bottom, 0.0, down(v[t]))
                - jnp.where(top, 0.0, up(above[t]))
            )
            south = jnp.where(bottom, 0.0, up(v[t]))
            north = jnp.where(top, 0.0, -down(above[t]))
            for m, value in enumerate((center, up(west_face), -down(east_face), south, north)):
                coef_ref[(at * BLOCKS + t) * 5 + m, pl.ds(0, groups), :] = value


def kernel(
    parts,
    count,
    groups,
    first_ref,
    second_ref,
    rate_ref,
    table_ref,
    flux_ref,
    nat_ref,
    out_ref,
    own_ref,
    west_ref,
    east_ref,
    stage_ref,
    flux_own,
    flux_west,
    flux_east,
    coef_ref,
    c_ref,
    w_ref,
    x_send,
    x_recv,
    w_send,
    w_recv,
    e_send,
    e_recv,
    r_send,
    r_recv,
    load_sem,
    save_sem,
    f_send,
    f_recv,
    f_load,
):
    region, me = lax.axis_index("region"), lax.axis_index("tracer")
    ring = lax.axis_size("region")
    east, west = (region + 1) % ring, (region + ring - 1) % ring
    reactions = first_ref.shape[0]
    species = parts * count
    rows = count * ROWS

    def partner(shift):
        return (me + shift) % parts

    barrier = pltpu.get_barrier_semaphore()
    for shift in range(1, parts):
        pl.semaphore_signal(barrier, 1, device_id=(region, partner(shift)), device_id_type=MESH)
    for side in (east, west):
        pl.semaphore_signal(barrier, 1, device_id=(side, me), device_id_type=MESH)
    pl.semaphore_wait(barrier, parts + 1)

    def remote(source, target, send, recv, device):
        return pltpu.make_async_remote_copy(
            src_ref=source,
            dst_ref=target,
            send_sem=send,
            recv_sem=recv,
            device_id=device,
            device_id_type=MESH,
        )

    def flux_east_copy():
        return remote(flux_ref, flux_west, f_send.at[0], f_recv.at[0], (east, me))

    def flux_west_copy():
        return remote(flux_ref, flux_east, f_send.at[1], f_recv.at[1], (west, me))

    def load(g):
        return pltpu.make_async_copy(nat_ref.at[:, me * groups + g], own_ref.at[0, g], load_sem.at[g])

    def exchange(shift, g):
        owner = partner(shift)
        return remote(
            nat_ref.at[:, owner * groups + g],
            own_ref.at[shift, g],
            x_send.at[shift, g],
            x_recv.at[shift, g],
            (region, owner),
        )

    def halo(part, g):
        source = nat_ref.at[:, me * groups + g] if part == 0 else own_ref.at[part, g]
        return (
            remote(source, west_ref.at[part, g], w_send.at[part, g], w_recv.at[part, g], (east, me)),
            remote(source, east_ref.at[part, g], e_send.at[part, g], e_recv.at[part, g], (west, me)),
        )

    def give_back(shift, g):
        return remote(
            stage_ref.at[shift, g],
            out_ref.at[:, me * groups + g],
            r_send.at[shift, g],
            r_recv.at[shift, g],
            (region, (me + parts - shift) % parts),
        )

    def save(g):
        return pltpu.make_async_copy(stage_ref.at[0, g], out_ref.at[:, me * groups + g], save_sem.at[g])

    def send_halo(part, g):
        for copy in halo(part, g):
            copy.start()

    def pass_on(g):
        for shift in range(1, parts):
            exchange(shift, g).wait_recv()
            send_halo(shift, g)

    flux_load = pltpu.make_async_copy(flux_ref, flux_own, f_load)
    flux_load.start()
    flux_east_copy().start()
    flux_west_copy().start()
    for g in range(groups):
        for shift in range(1, parts):
            exchange(shift, g).start()
        if g < 2:
            send_halo(0, g)
    for g in range(groups):
        load(g).start()
    c_ref[...] = jnp.zeros_like(c_ref)
    flux_load.wait()
    flux_east_copy().wait()
    flux_west_copy().wait()
    write_coefficients(groups, coef_ref, flux_own, flux_west, flux_east)
    for g in range(2):
        if g < groups:
            pass_on(g)
        if g + 2 < groups:
            send_halo(0, g + 2)

    lane = lax.broadcasted_iota(jnp.int32, (8, LANES), 1)
    unroll = 16

    def one_group(g, carry):
        @pl.when(g + 2 < groups)
        def _():
            pass_on(g + 2)

        @pl.when(g + 4 < groups)
        def _():
            send_halo(0, g + 4)

        load(g).wait()
        for part in range(parts):
            for copy in halo(part, g):
                copy.wait_recv()

        def coefficient(at, t, m):
            return coef_ref[(at * BLOCKS + t) * 5 + m, pl.ds(g, 8, stride=0), :]

        def step(cols, at):
            south, north = south_of(cols[1], lane), north_of(cols[1], lane)
            return [
                coefficient(at, t, 0) * cols[1][t]
                + coefficient(at, t, 1) * cols[0][t]
                + coefficient(at, t, 2) * cols[2][t]
                + coefficient(at, t, 3) * south[t]
                + coefficient(at, t, 4) * north[t]
                for t in range(BLOCKS)
            ]

        for part in range(parts):

            def advect(i, carry, part=part):
                def read(ref, column):
                    flat = ref.at[part, g].reshape(rows, LANES)
                    return [
                        flat[pl.ds(i * (8 * ROWS) + t * COLUMNS + column, 8, stride=ROWS), :]
                        for t in range(BLOCKS)
                    ]

                cols = [read(ref, column) for ref in (west_ref, own_ref, east_ref) for column in range(2)]
                mid = [step(cols[at : at + 3], at) for at in range(4)]
                for column in range(COLUMNS):
                    new = step(mid[column : column + 3], column + 1)
                    for t in range(BLOCKS):
                        start = (part * count + i * 8) * PITCH + t * COLUMNS + column
                        c_ref[pl.ds(start, 8, stride=PITCH), :] = new[t]
                return carry

            lax.fori_loop(0, count // 8, advect, 0)

        def react(repeat, carry):
            def velocities(i, carry):
                for j in range(unroll):
                    r = i * unroll + j
                    w_ref[pl.ds(r * PITCH, 8), :] = (
                        rate_ref[r]
                        * c_ref[pl.ds(first_ref[r], 8), :]
                        * c_ref[pl.ds(second_ref[r], 8), :]
                    )
                return carry

            lax.fori_loop(0, reactions // unroll, velocities, 0)

            for k in range(ROWS):
                w = w_ref[pl.ds(k, reactions, stride=PITCH), :]
                high = w.astype(jnp.bfloat16)
                low = (w - high.astype(jnp.float32)).astype(jnp.bfloat16)
                change = jnp.dot(
                    table_ref[...],
                    jnp.concatenate([high, low], axis=1),
                    preferred_element_type=jnp.float32,
                )
                where = pl.ds(k, species, stride=PITCH)
                c_ref[where, :] = c_ref[where, :] + (change[:, :LANES] + change[:, LANES:])
            return carry

        lax.fori_loop(0, SUBSTEPS, react, 0)

        for part in range(parts):

            def put(i, carry, part=part):
                flat = stage_ref.at[part, g].reshape(rows, LANES)
                for k in range(ROWS):
                    start = (part * count + i * 8) * PITCH + k
                    flat[pl.ds(i * (8 * ROWS) + k, 8, stride=ROWS), :] = c_ref[
                        pl.ds(start, 8, stride=PITCH), :
                    ]
                return carry

            lax.fori_loop(0, count // 8, put, 0)
        for shift in range(1, parts):
            give_back(shift, g).start()
        save(g).start()
        return carry

    lax.fori_loop(0, groups, one_group, 0)

    def finish(g, carry):
        save(g).wait()
        for shift in range(1, parts):
            exchange(shift, g).wait_send()
            give_back(shift, g).wait()
        for part in range(parts):
            for copy in halo(part, g):
                copy.wait_send()
        return carry

    lax.fori_loop(0, groups, finish, 0)


def body(tracers, fluxes, rate_coeff, first_reactant, second_reactant, product_species):
    parts = lax.axis_size("tracer")
    me = lax.axis_index("tracer")
    count, columns, length = tracers.shape
    total = length // GROUP
    groups = total // parts
    species = parts * count
    reactions = rate_coeff.shape[0]

    def by_block(values):
        lead = values.shape[0]
        blocks = values.shape[2] // LANES
        return (
            values.reshape(lead, columns, blocks, LANES)
            .transpose(0, 2, 1, 3)
            .reshape(lead, blocks // BLOCKS, BLOCKS, columns, LANES)
        )

    natural = by_block(tracers)
    wind = by_block(fluxes)

    def place(index):
        return (me - index // count) % parts * count + index % count

    order = jnp.arange(species, dtype=jnp.int32)[:, None]
    first, second, product = (
        place(index) for index in (first_reactant, second_reactant, product_species)
    )
    table = (
        (product[None, :] == order).astype(jnp.float32)
        - (first[None, :] == order).astype(jnp.float32)
        - (second[None, :] == order).astype(jnp.float32)
    ).astype(jnp.bfloat16)

    smem = pl.BlockSpec(memory_space=pltpu.SMEM)
    vmem = pl.BlockSpec(memory_space=pltpu.VMEM)
    anywhere = pl.BlockSpec(memory_space=pl.ANY)
    slab = (parts, groups, count, BLOCKS, columns, LANES)
    dma = pltpu.SemaphoreType.DMA
    out = pl.pallas_call(
        functools.partial(kernel, parts, count, groups),
        out_shape=jax.ShapeDtypeStruct(natural.shape, jnp.float32),
        in_specs=[smem] * 3 + [vmem] + [anywhere] * 2,
        out_specs=anywhere,
        scratch_shapes=[pltpu.VMEM(slab, jnp.float32)] * 4
        + [pltpu.VMEM(wind.shape, jnp.float32)] * 3
        + [
            pltpu.VMEM((4 * BLOCKS * 5, -(-groups // 8) * 8, LANES), jnp.float32),
            pltpu.VMEM((species * PITCH + 8, LANES), jnp.float32),
            pltpu.VMEM((reactions * PITCH + 8, LANES), jnp.float32),
        ]
        + [dma((parts, groups))] * 8
        + [dma((groups,))] * 2
        + [dma((2,))] * 2
        + [dma(())],
        compiler_params=pltpu.CompilerParams(
            vmem_limit_bytes=56 * 1024 * 1024, collective_id=0, has_side_effects=True
        ),
        name="belt",
    )(first * PITCH, second * PITCH, rate_coeff, table, wind, natural)
    return (
        out.reshape(count, total * BLOCKS, columns, LANES).transpose(0, 2, 1, 3).reshape(tracers.shape)
    )


def solution(mesh):
    in_specs = (P("tracer", "region", None), P(None, "region", "tracer"), P(), P(), P(), P())
    out_specs = P("tracer", "region", None)
    return jax.shard_map(body, mesh=mesh, in_specs=in_specs, out_specs=out_specs, check_vma=False)
```

```python
import functools

import jax
import jax.numpy as jnp
from jax import lax
from jax.experimental import pallas as pl
from jax.experimental.pallas import tpu as pltpu
from jax.sharding import PartitionSpec as P

NY = 48
SUBSTEPS = 4
LANES = 128
BLOCKS = 3
COLUMNS = 2
ROWS = COLUMNS * BLOCKS
GROUP = BLOCKS * LANES
SIDES = 2
STRIP = SIDES * ROWS
PITCH = STRIP + 1
UNROLL = 16
MESH = pl.DeviceIdType.MESH


def south_of(values, lane):
    shifted = []
    for t in range(BLOCKS):
        source = values[t] if t == 0 else jnp.where(lane == LANES - 1, values[t - 1], values[t])
        shifted.append(pltpu.roll(source, 1, 1))
    return shifted


def north_of(values, lane):
    shifted = []
    for t in range(BLOCKS):
        last = t == BLOCKS - 1
        source = values[t] if last else jnp.where(lane == 0, values[t + 1], values[t])
        shifted.append(pltpu.roll(source, LANES - 1, 1))
    return shifted


def up(values):
    return jnp.maximum(values, 0.0)


def down(values):
    return jnp.minimum(values, 0.0)


def write_coefficients(groups, coef_ref, own_ref, west_ref, east_ref):
    lane = lax.broadcasted_iota(jnp.int32, (groups, LANES), 1)

    def read(ref, axis, column):
        rows = ref.reshape(2 * groups * ROWS, LANES)
        return [
            rows[pl.ds(axis * groups * ROWS + t * COLUMNS + column, groups, stride=ROWS), :]
            for t in range(BLOCKS)
        ]

    sources = [(west_ref, COLUMNS - 1)]
    sources += [(own_ref.at[side], column) for side in range(SIDES) for column in range(COLUMNS)]
    sources += [(east_ref, 0), (east_ref, 1)]
    u = [read(ref, 0, column) for ref, column in sources]
    for at in range(len(sources) - 1):
        v = read(sources[at][0], 1, sources[at][1])
        above = north_of(v, lane)
        for t in range(BLOCKS):
            y = (lane + t * LANES) % NY
            bottom, top = y == 0, y == NY - 1
            west_face, east_face = u[at][t], u[at + 1][t]
            center = (
                1.0
                + down(west_face)
                - up(east_face)
                + jnp.where(bottom, 0.0, down(v[t]))
                - jnp.where(top, 0.0, up(above[t]))
            )
            south = jnp.where(bottom, 0.0, up(v[t]))
            north = jnp.where(top, 0.0, -down(above[t]))
            for m, value in enumerate((center, up(west_face), -down(east_face), south, north)):
                coef_ref[(at * BLOCKS + t) * 5 + m, pl.ds(0, groups), :] = value


def kernel(
    parts,
    count,
    groups,
    first_ref,
    second_ref,
    rate_ref,
    first_row,
    second_row,
    product_row,
    flux_ref,
    nat_ref,
    out_ref,
    own_ref,
    stage_ref,
    west_ref,
    east_ref,
    flux_own,
    flux_west,
    flux_east,
    coef_ref,
    now_ref,
    c_ref,
    w_ref,
    k_ref,
    table_ref,
    first_at,
    second_at,
    g_send,
    g_recv,
    r_send,
    r_recv,
    w_send,
    w_recv,
    e_send,
    e_recv,
    f_send,
    f_recv,
    fh_send,
    fh_recv,
):
    region, me = lax.axis_index("region"), lax.axis_index("tracer")
    strips = lax.axis_size("region") // SIDES
    quad, bit, side = region // 4, (region // 2) % 2, region % 2
    strip = quad * 2 + side
    home = side == bit
    reactions = first_ref.shape[0]
    species = parts * count
    rows = count * ROWS

    def seat(at, b):
        return (at // 2) * 4 + b * 2 + at % 2

    west, east = seat((strip + strips - 1) % strips, bit), seat((strip + 1) % strips, bit)
    outer = jnp.where(side == 0, west, east)

    barrier = pltpu.get_barrier_semaphore()
    for shift in range(parts):
        for d in range(2):
            for e in range(2):
                if shift or d or e:
                    pl.semaphore_signal(
                        barrier,
                        1,
                        device_id=(quad * 4 + (bit + d) % 2 * 2 + (side + e) % 2, (me + shift) % parts),
                        device_id_type=MESH,
                    )
    pl.semaphore_signal(barrier, 1, device_id=(outer, me), device_id_type=MESH)
    pl.semaphore_wait(barrier, 4 * parts)

    def remote(source, target, send, recv, device):
        return pltpu.make_async_remote_copy(
            src_ref=source,
            dst_ref=target,
            send_sem=send,
            recv_sem=recv,
            device_id=device,
            device_id_type=MESH,
        )

    def start(copy_here, copy_there, maybe_here):
        if maybe_here:

            @pl.when(home)
            def _():
                copy_here().start()

            @pl.when(jnp.logical_not(home))
            def _():
                copy_there().start()

        else:
            copy_there().start()

    def sent(copy_there, maybe_here):
        if maybe_here:

            @pl.when(jnp.logical_not(home))
            def _():
                copy_there().wait_send()

        else:
            copy_there().wait_send()

    def gather(shift, d, g):
        owner, half = (me + shift) % parts, (bit + d) % 2
        source = nat_ref.at[:, (owner * 2 + half) * groups + g]
        target, arrived = own_ref.at[me, side, g], g_recv.at[me, side, g]
        return (
            lambda: pltpu.make_async_copy(source, target, arrived),
            lambda: remote(source, target, g_send.at[shift, d, g], arrived, (seat(quad * 2 + bit, half), owner)),
            shift == 0 and d == 0,
        )

    def gathered(part, s, g):
        return remote(
            own_ref.at[part, s, g], own_ref.at[part, s, g], g_send.at[0, 0, g], g_recv.at[part, s, g], (east, me)
        )

    def to_west(part, g):
        return remote(
            own_ref.at[part, 0, g], east_ref.at[part, g], e_send.at[part, g], e_recv.at[part, g], (west, me)
        )

    def to_east(part, g):
        return remote(
            own_ref.at[part, 1, g], west_ref.at[part, g], w_send.at[part, g], w_recv.at[part, g], (east, me)
        )

    def give_back(shift, e, g):
        part, s = (me + parts - shift) % parts, (side + e) % 2
        source, target = stage_ref.at[part, s, g], out_ref.at[:, (me * 2 + bit) * groups + g]
        arrived = r_recv.at[shift, (bit + side) % 2, g]
        return (
            lambda: pltpu.make_async_copy(source, target, arrived),
            lambda: remote(source, target, r_send.at[shift, e, g], arrived, (quad * 4 + side * 2 + s, part)),
            shift == 0 and e == 0,
        )

    def returned(shift, d, g):
        target = out_ref.at[:, g]
        return remote(stage_ref.at[0, 0, g], target, r_send.at[0, 0, g], r_recv.at[shift, d, g], (east, me))

    pairs = [(shift, d) for shift in (*range(1, parts), 0) for d in (1, 0)]

    def flux_gather(d):
        half = (bit + d) % 2
        source = flux_ref.at[:, pl.ds(half * groups, groups)]
        target, arrived = flux_own.at[side], f_recv.at[side]
        return (
            lambda: pltpu.make_async_copy(source, target, arrived),
            lambda: remote(source, target, f_send.at[d], arrived, (seat(quad * 2 + bit, half), me)),
            d == 0,
        )

    def flux_gathered(s):
        return remote(flux_own.at[s], flux_own.at[s], f_send.at[0], f_recv.at[s], (east, me))

    def flux_halo():
        return (
            remote(flux_own.at[0], flux_east, fh_send.at[0], fh_recv.at[0], (west, me)),
            remote(flux_own.at[1], flux_west, fh_send.at[1], fh_recv.at[1], (east, me)),
        )

    def pass_on(g):
        for shift in range(parts):
            part = (me + shift) % parts
            for s, onward in ((0, to_west), (1, to_east)):
                gathered(part, s, g).wait_recv()
                onward(part, g).start()

    for d in (1, 0):
        start(*flux_gather(d))
    for g in range(groups):
        for pair in pairs:
            start(*gather(*pair, g))

    def prepare(r, carry):
        first_at[r] = first_ref[r] * PITCH
        second_at[r] = second_ref[r] * PITCH
        k_ref[pl.ds(r, 1), :] = jnp.full((1, LANES), rate_ref[r], jnp.float32)
        return carry

    lax.fori_loop(0, reactions, prepare, 0)

    def build(i, carry):
        at = pl.multiple_of(i * 16, 16)
        order = lax.broadcasted_iota(jnp.int32, (16, reactions), 0) + at
        table_ref[pl.ds(at, 16), :] = (
            (product_row[...] == order).astype(jnp.float32)
            - (first_row[...] == order).astype(jnp.float32)
            - (second_row[...] == order).astype(jnp.float32)
        ).astype(jnp.bfloat16)
        return carry

    lax.fori_loop(0, species // 16, build, 0)

    for s in range(SIDES):
        flux_gathered(s).wait_recv()
    for copy in flux_halo():
        copy.start()
    for copy in flux_halo():
        copy.wait()
    for d in (1, 0):
        _, there, maybe_here = flux_gather(d)
        sent(there, maybe_here)
    write_coefficients(groups, coef_ref, flux_own, flux_west, flux_east)
    pass_on(0)

    lane = lax.broadcasted_iota(jnp.int32, (8, LANES), 1)
    batch = max(b for b in (1, 2, 4) if count % (8 * b) == 0)

    def one_group(g, carry):
        def spread(i, carry):
            now_ref[i, :, :] = coef_ref[i, pl.ds(g, 8, stride=0), :]
            return carry

        lax.fori_loop(0, coef_ref.shape[0], spread, 0)
        for part in range(parts):
            to_west(part, g).wait_recv()
            to_east(part, g).wait_recv()

        def step(cols, at, shifted):
            south, north = shifted
            return [
                now_ref[(at * BLOCKS + t) * 5, :, :] * cols[1][t]
                + now_ref[(at * BLOCKS + t) * 5 + 1, :, :] * cols[0][t]
                + now_ref[(at * BLOCKS + t) * 5 + 2, :, :] * cols[2][t]
                + now_ref[(at * BLOCKS + t) * 5 + 3, :, :] * south[t]
                + now_ref[(at * BLOCKS + t) * 5 + 4, :, :] * north[t]
                for t in range(BLOCKS)
            ]

        width = SIDES * COLUMNS
        for part in range(parts):
            slabs = [west_ref.at[part, g]]
            slabs += [own_ref.at[part, s, g] for s in range(SIDES)]
            slabs += [east_ref.at[part, g]]

            def advect(i, carry, part=part, slabs=slabs):
                def read(slab, column, block):
                    flat = slab.reshape(rows, LANES)
                    return [
                        flat[pl.ds(block * (8 * ROWS) + t * COLUMNS + column, 8, stride=ROWS), :]
                        for t in range(BLOCKS)
                    ]

                def shifts(values):
                    return south_of(values, lane), north_of(values, lane)

                blocks = [i * batch + j for j in range(batch)]
                cols = [
                    [read(slab, column, block) for slab in slabs for column in range(COLUMNS)]
                    for block in blocks
                ]
                moved = [[shifts(c[at + 1]) for at in range(width + 2)] for c in cols]
                mid = [
                    [step(c[at : at + 3], at, m[at]) for at in range(width + 2)]
                    for c, m in zip(cols, moved)
                ]
                moved = [[shifts(c[at + 1]) for at in range(width)] for c in mid]
                for block, c, m in zip(blocks, mid, moved):
                    for at in range(width):
                        new = step(c[at : at + 3], at + 1, m[at])
                        for t in range(BLOCKS):
                            place = at // COLUMNS * ROWS + t * COLUMNS + at % COLUMNS
                            begin = (part * count + block * 8) * PITCH + place
                            c_ref[pl.ds(begin, 8, stride=PITCH), :] = new[t]
                return carry

            lax.fori_loop(0, count // (8 * batch), advect, 0)

        @pl.when(g + 1 < groups)
        def _():
            pass_on(g + 1)

        def react(repeat, carry):
            def velocities(i, carry):
                for j in range(UNROLL):
                    r = i * UNROLL + j
                    one, two = first_at[r], second_at[r]
                    for at in (0, STRIP - 8):
                        w_ref[pl.ds(r * PITCH + at, 8), :] = (
                            c_ref[pl.ds(one + at, 8), :] * c_ref[pl.ds(two + at, 8), :]
                        )
                return carry

            lax.fori_loop(0, reactions // UNROLL, velocities, 0)

            for k in range(STRIP):
                w = w_ref[pl.ds(k, reactions, stride=PITCH), :] * k_ref[...]
                high = w.astype(jnp.bfloat16)
                low = (w - high.astype(jnp.float32)).astype(jnp.bfloat16)
                change = jnp.dot(
                    table_ref[...],
                    jnp.concatenate([high, low], axis=1),
                    preferred_element_type=jnp.float32,
                )
                where = pl.ds(k, species, stride=PITCH)
                c_ref[where, :] = c_ref[where, :] + (change[:, :LANES] + change[:, LANES:])
            return carry

        lax.fori_loop(0, SUBSTEPS, react, 0)

        for part in range(parts):

            def put(i, carry, part=part):
                for s in range(SIDES):
                    flat = stage_ref.at[part, s, g].reshape(rows, LANES)
                    for k in range(ROWS):
                        begin = (part * count + i * 8) * PITCH + s * ROWS + k
                        flat[pl.ds(i * (8 * ROWS) + k, 8, stride=ROWS), :] = c_ref[
                            pl.ds(begin, 8, stride=PITCH), :
                        ]
                return carry

            lax.fori_loop(0, count // 8, put, 0)
        for pair in pairs:
            start(*give_back(*pair, g))
        return carry

    lax.fori_loop(0, groups, one_group, 0)

    def finish(g, carry):
        for pair in pairs:
            for _, there, maybe_here in (gather(*pair, g), give_back(*pair, g)):
                sent(there, maybe_here)
            returned(*pair, g).wait_recv()
        for part in range(parts):
            to_west(part, g).wait_send()
            to_east(part, g).wait_send()
        return carry

    lax.fori_loop(0, groups, finish, 0)


def body(tracers, fluxes, rate_coeff, first_reactant, second_reactant, product_species):
    parts = lax.axis_size("tracer")
    count, columns, length = tracers.shape
    total = length // GROUP
    groups = total // (2 * parts)
    species = parts * count
    reactions = rate_coeff.shape[0]

    def by_block(values):
        lead = values.shape[0]
        blocks = values.shape[2] // LANES
        return (
            values.reshape(lead, columns, blocks, LANES)
            .transpose(0, 2, 1, 3)
            .reshape(lead, blocks // BLOCKS, BLOCKS, columns, LANES)
        )

    natural = by_block(tracers)
    smem = pl.BlockSpec(memory_space=pltpu.SMEM)
    vmem = pl.BlockSpec(memory_space=pltpu.VMEM)
    anywhere = pl.BlockSpec(memory_space=pl.ANY)
    tile = (BLOCKS, columns, LANES)
    f32 = jnp.float32
    dma = pltpu.SemaphoreType.DMA
    coefs = (SIDES * columns + 2) * BLOCKS * 5
    out = pl.pallas_call(
        functools.partial(kernel, parts, count, groups),
        out_shape=jax.ShapeDtypeStruct(natural.shape, f32),
        in_specs=[smem] * 3 + [vmem] * 3 + [anywhere] * 2,
        out_specs=anywhere,
        scratch_shapes=[pltpu.VMEM((parts, SIDES, groups, count, *tile), f32)] * 2
        + [pltpu.VMEM((parts, groups, count, *tile), f32)] * 2
        + [pltpu.VMEM((SIDES, 2, groups, *tile), f32)]
        + [pltpu.VMEM((2, groups, *tile), f32)] * 2
        + [
            pltpu.VMEM((coefs, -(-groups // 8) * 8, LANES), f32),
            pltpu.VMEM((coefs, 8, LANES), f32),
            pltpu.VMEM((species * PITCH + 8, LANES), f32),
            pltpu.VMEM((reactions * PITCH + 8, LANES), f32),
            pltpu.VMEM((reactions, LANES), f32),
            pltpu.VMEM((species, reactions), jnp.bfloat16),
            pltpu.SMEM((reactions,), jnp.int32),
            pltpu.SMEM((reactions,), jnp.int32),
        ]
        + [dma((parts, 2, groups))] * 4
        + [dma((parts, groups))] * 4
        + [dma((2,))] * 4,
        compiler_params=pltpu.CompilerParams(
            vmem_limit_bytes=56 * 1024 * 1024, collective_id=0, has_side_effects=True
        ),
        name="belt",
    )(
        first_reactant,
        second_reactant,
        rate_coeff,
        first_reactant[None, :],
        second_reactant[None, :],
        product_species[None, :],
        by_block(fluxes),
        natural,
    )
    return (
        out.reshape(count, total * BLOCKS, columns, LANES).transpose(0, 2, 1, 3).reshape(tracers.shape)
    )


def solution(mesh):
    in_specs = (P("tracer", "region", None), P(None, "region", "tracer"), P(), P(), P(), P())
    out_specs = P("tracer", "region", None)
    return jax.shard_map(body, mesh=mesh, in_specs=in_specs, out_specs=out_specs, check_vma=False)
```

```python
import functools

import jax
import jax.numpy as jnp
from jax import lax
from jax.experimental import pallas as pl
from jax.experimental.pallas import tpu as pltpu
from jax.sharding import PartitionSpec as P

NY = 48
SUBSTEPS = 4
LANES = 128
BLOCKS = 3
COLUMNS = 2
ROWS = COLUMNS * BLOCKS
GROUP = BLOCKS * LANES
SIDES = 2
STRIP = SIDES * ROWS
PITCH = STRIP + 1
UNROLL = 32
MESH = pl.DeviceIdType.MESH


def south_of(values, lane):
    shifted = []
    for t in range(BLOCKS):
        source = values[t] if t == 0 else jnp.where(lane == LANES - 1, values[t - 1], values[t])
        shifted.append(pltpu.roll(source, 1, 1))
    return shifted


def north_of(values, lane):
    shifted = []
    for t in range(BLOCKS):
        last = t == BLOCKS - 1
        source = values[t] if last else jnp.where(lane == 0, values[t + 1], values[t])
        shifted.append(pltpu.roll(source, LANES - 1, 1))
    return shifted


def up(values):
    return jnp.maximum(values, 0.0)


def down(values):
    return jnp.minimum(values, 0.0)


def write_coefficients(groups, coef_ref, own_ref, west_ref, east_ref):
    lane = lax.broadcasted_iota(jnp.int32, (groups, LANES), 1)

    def read(ref, axis, column):
        rows = ref.reshape(2 * groups * ROWS, LANES)
        return [
            rows[pl.ds(axis * groups * ROWS + t * COLUMNS + column, groups, stride=ROWS), :]
            for t in range(BLOCKS)
        ]

    sources = [(west_ref, COLUMNS - 1)]
    sources += [(own_ref.at[side], column) for side in range(SIDES) for column in range(COLUMNS)]
    sources += [(east_ref, 0), (east_ref, 1)]
    u = [read(ref, 0, column) for ref, column in sources]
    for at in range(len(sources) - 1):
        v = read(sources[at][0], 1, sources[at][1])
        above = north_of(v, lane)
        for t in range(BLOCKS):
            y = (lane + t * LANES) % NY
            bottom, top = y == 0, y == NY - 1
            west_face, east_face = u[at][t], u[at + 1][t]
            center = (
                1.0
                + down(west_face)
                - up(east_face)
                + jnp.where(bottom, 0.0, down(v[t]))
                - jnp.where(top, 0.0, up(above[t]))
            )
            south = jnp.where(bottom, 0.0, up(v[t]))
            north = jnp.where(top, 0.0, -down(above[t]))
            for m, value in enumerate((center, up(west_face), -down(east_face), south, north)):
                coef_ref[(at * BLOCKS + t) * 5 + m, pl.ds(0, groups), :] = value


def kernel(
    parts,
    count,
    groups,
    first_ref,
    second_ref,
    rate_ref,
    first_row,
    second_row,
    product_row,
    flux_ref,
    nat_ref,
    out_ref,
    own_ref,
    stage_ref,
    west_ref,
    east_ref,
    flux_own,
    flux_west,
    flux_east,
    coef_ref,
    now_ref,
    c_ref,
    w_ref,
    k_ref,
    table_ref,
    first_at,
    second_at,
    g_send,
    g_recv,
    r_send,
    r_recv,
    w_send,
    w_recv,
    e_send,
    e_recv,
    f_send,
    f_recv,
    fh_send,
    fh_recv,
):
    region, me = lax.axis_index("region"), lax.axis_index("tracer")
    strips = lax.axis_size("region") // SIDES
    quad, bit, side = region // 4, (region // 2) % 2, region % 2
    strip = quad * 2 + side
    home = side == bit
    reactions = first_ref.shape[0]
    species = parts * count
    rows = count * ROWS

    def seat(at, b):
        return (at // 2) * 4 + b * 2 + at % 2

    west, east = seat((strip + strips - 1) % strips, bit), seat((strip + 1) % strips, bit)
    outer = jnp.where(side == 0, west, east)

    barrier = pltpu.get_barrier_semaphore()
    for shift in range(parts):
        for d in range(2):
            for e in range(2):
                if shift or d or e:
                    pl.semaphore_signal(
                        barrier,
                        1,
                        device_id=(quad * 4 + (bit + d) % 2 * 2 + (side + e) % 2, (me + shift) % parts),
                        device_id_type=MESH,
                    )
    pl.semaphore_signal(barrier, 1, device_id=(outer, me), device_id_type=MESH)
    pl.semaphore_wait(barrier, 4 * parts)

    def remote(source, target, send, recv, device):
        return pltpu.make_async_remote_copy(
            src_ref=source,
            dst_ref=target,
            send_sem=send,
            recv_sem=recv,
            device_id=device,
            device_id_type=MESH,
        )

    def start(copy_here, copy_there, maybe_here):
        if maybe_here:

            @pl.when(home)
            def _():
                copy_here().start()

            @pl.when(jnp.logical_not(home))
            def _():
                copy_there().start()

        else:
            copy_there().start()

    def sent(copy_there, maybe_here):
        if maybe_here:

            @pl.when(jnp.logical_not(home))
            def _():
                copy_there().wait_send()

        else:
            copy_there().wait_send()

    def gather(shift, d, g):
        owner, half = (me + shift) % parts, (bit + d) % 2
        source = nat_ref.at[:, (owner * 2 + half) * groups + g]
        target, arrived = own_ref.at[me, side, g], g_recv.at[me, side, g]
        return (
            lambda: pltpu.make_async_copy(source, target, arrived),
            lambda: remote(source, target, g_send.at[shift, d, g], arrived, (seat(quad * 2 + bit, half), owner)),
            shift == 0 and d == 0,
        )

    def gathered(part, s, g):
        return remote(
            own_ref.at[part, s, g], own_ref.at[part, s, g], g_send.at[0, 0, g], g_recv.at[part, s, g], (east, me)
        )

    def to_west(part, g):
        return remote(
            own_ref.at[part, 0, g], east_ref.at[part, g], e_send.at[part, g], e_recv.at[part, g], (west, me)
        )

    def to_east(part, g):
        return remote(
            own_ref.at[part, 1, g], west_ref.at[part, g], w_send.at[part, g], w_recv.at[part, g], (east, me)
        )

    def give_back(shift, e, g):
        part, s = (me + parts - shift) % parts, (side + e) % 2
        source, target = stage_ref.at[part, s, g], out_ref.at[:, (me * 2 + bit) * groups + g]
        arrived = r_recv.at[shift, (bit + side) % 2, g]
        return (
            lambda: pltpu.make_async_copy(source, target, arrived),
            lambda: remote(source, target, r_send.at[shift, e, g], arrived, (quad * 4 + side * 2 + s, part)),
            shift == 0 and e == 0,
        )

    def returned(shift, d, g):
        target = out_ref.at[:, g]
        return remote(stage_ref.at[0, 0, g], target, r_send.at[0, 0, g], r_recv.at[shift, d, g], (east, me))

    pairs = [(shift, d) for shift in (*range(1, parts), 0) for d in (1, 0)]

    def flux_gather(d):
        half = (bit + d) % 2
        source = flux_ref.at[:, pl.ds(half * groups, groups)]
        target, arrived = flux_own.at[side], f_recv.at[side]
        return (
            lambda: pltpu.make_async_copy(source, target, arrived),
            lambda: remote(source, target, f_send.at[d], arrived, (seat(quad * 2 + bit, half), me)),
            d == 0,
        )

    def flux_gathered(s):
        return remote(flux_own.at[s], flux_own.at[s], f_send.at[0], f_recv.at[s], (east, me))

    def flux_halo():
        return (
            remote(flux_own.at[0], flux_east, fh_send.at[0], fh_recv.at[0], (west, me)),
            remote(flux_own.at[1], flux_west, fh_send.at[1], fh_recv.at[1], (east, me)),
        )

    def pass_on(g):
        for shift in range(parts):
            part = (me + shift) % parts
            for s, onward in ((0, to_west), (1, to_east)):
                gathered(part, s, g).wait_recv()
                onward(part, g).start()

    for d in (1, 0):
        start(*flux_gather(d))
    straight = [pair for pair in pairs if pair[0] and not pair[1]]
    far = [pair for pair in pairs if pair[0] and pair[1]]
    for g in range(groups):

        @pl.when(side == 0)
        def _(g=g):
            for pair in far + straight:
                start(*gather(*pair, g))

        @pl.when(side != 0)
        def _(g=g):
            for pair in straight + far:
                start(*gather(*pair, g))

        for pair in pairs:
            if pair not in far and pair not in straight:
                start(*gather(*pair, g))

    def prepare(r, carry):
        first_at[r] = first_ref[r] * PITCH
        second_at[r] = second_ref[r] * PITCH
        k_ref[pl.ds(r, 1), :] = jnp.full((1, LANES), rate_ref[r], jnp.float32)
        return carry

    lax.fori_loop(0, reactions, prepare, 0)

    def build(i, carry):
        at = pl.multiple_of(i * 16, 16)
        order = lax.broadcasted_iota(jnp.int32, (16, reactions), 0) + at
        table_ref[pl.ds(at, 16), :] = (
            (product_row[...] == order).astype(jnp.float32)
            - (first_row[...] == order).astype(jnp.float32)
            - (second_row[...] == order).astype(jnp.float32)
        ).astype(jnp.bfloat16)
        return carry

    lax.fori_loop(0, species // 16, build, 0)

    for s in range(SIDES):
        flux_gathered(s).wait_recv()
    for copy in flux_halo():
        copy.start()
    for copy in flux_halo():
        copy.wait()
    for d in (1, 0):
        _, there, maybe_here = flux_gather(d)
        sent(there, maybe_here)
    write_coefficients(groups, coef_ref, flux_own, flux_west, flux_east)
    pass_on(0)

    lane = lax.broadcasted_iota(jnp.int32, (8, LANES), 1)
    batch = max(b for b in (1, 2, 4) if count % (8 * b) == 0)

    def one_group(g, carry):
        def spread(i, carry):
            now_ref[i, :, :] = coef_ref[i, pl.ds(g, 8, stride=0), :]
            return carry

        lax.fori_loop(0, coef_ref.shape[0], spread, 0)
        for part in range(parts):
            to_west(part, g).wait_recv()
            to_east(part, g).wait_recv()

        def step(cols, at, shifted):
            south, north = shifted
            return [
                now_ref[(at * BLOCKS + t) * 5, :, :] * cols[1][t]
                + now_ref[(at * BLOCKS + t) * 5 + 1, :, :] * cols[0][t]
                + now_ref[(at * BLOCKS + t) * 5 + 2, :, :] * cols[2][t]
                + now_ref[(at * BLOCKS + t) * 5 + 3, :, :] * south[t]
                + now_ref[(at * BLOCKS + t) * 5 + 4, :, :] * north[t]
                for t in range(BLOCKS)
            ]

        width = SIDES * COLUMNS
        for part in range(parts):
            slabs = [west_ref.at[part, g]]
            slabs += [own_ref.at[part, s, g] for s in range(SIDES)]
            slabs += [east_ref.at[part, g]]

            def advect(i, carry, part=part, slabs=slabs):
                def read(slab, column, block):
                    flat = slab.reshape(rows, LANES)
                    return [
                        flat[pl.ds(block * (8 * ROWS) + t * COLUMNS + column, 8, stride=ROWS), :]
                        for t in range(BLOCKS)
                    ]

                def shifts(values):
                    return south_of(values, lane), north_of(values, lane)

                blocks = [i * batch + j for j in range(batch)]
                cols = [
                    [read(slab, column, block) for slab in slabs for column in range(COLUMNS)]
                    for block in blocks
                ]
                moved = [[shifts(c[at + 1]) for at in range(width + 2)] for c in cols]
                mid = [
                    [step(c[at : at + 3], at, m[at]) for at in range(width + 2)]
                    for c, m in zip(cols, moved)
                ]
                moved = [[shifts(c[at + 1]) for at in range(width)] for c in mid]
                for block, c, m in zip(blocks, mid, moved):
                    for at in range(width):
                        new = step(c[at : at + 3], at + 1, m[at])
                        for t in range(BLOCKS):
                            place = at // COLUMNS * ROWS + t * COLUMNS + at % COLUMNS
                            begin = (part * count + block * 8) * PITCH + place
                            c_ref[pl.ds(begin, 8, stride=PITCH), :] = new[t]
                return carry

            lax.fori_loop(0, count // (8 * batch), advect, 0)

        @pl.when(g + 1 < groups)
        def _():
            pass_on(g + 1)

        def react(repeat, carry):
            def velocities(i, carry):
                for j in range(UNROLL):
                    r = i * UNROLL + j
                    one, two = first_at[r], second_at[r]
                    for at in (0, STRIP - 8):
                        w_ref[pl.ds(r * PITCH + at, 8), :] = (
                            c_ref[pl.ds(one + at, 8), :] * c_ref[pl.ds(two + at, 8), :]
                        )
                return carry

            lax.fori_loop(0, reactions // UNROLL, velocities, 0)

            for k in range(STRIP):
                w = w_ref[pl.ds(k, reactions, stride=PITCH), :] * k_ref[...]
                high = w.astype(jnp.bfloat16)
                low = (w - high.astype(jnp.float32)).astype(jnp.bfloat16)
                change = jnp.dot(
                    table_ref[...],
                    jnp.concatenate([high, low], axis=1),
                    preferred_element_type=jnp.float32,
                )
                where = pl.ds(k, species, stride=PITCH)
                c_ref[where, :] = c_ref[where, :] + (change[:, :LANES] + change[:, LANES:])
            return carry

        lax.fori_loop(0, SUBSTEPS, react, 0)

        for part in range(parts):

            def put(i, carry, part=part):
                for s in range(SIDES):
                    flat = stage_ref.at[part, s, g].reshape(rows, LANES)
                    for k in range(ROWS):
                        begin = (part * count + i * 8) * PITCH + s * ROWS + k
                        flat[pl.ds(i * (8 * ROWS) + k, 8, stride=ROWS), :] = c_ref[
                            pl.ds(begin, 8, stride=PITCH), :
                        ]
                return carry

            lax.fori_loop(0, count // 8, put, 0)
        for pair in pairs:
            start(*give_back(*pair, g))
        return carry

    lax.fori_loop(0, groups, one_group, 0)

    def finish(g, carry):
        for pair in pairs:
            for _, there, maybe_here in (gather(*pair, g), give_back(*pair, g)):
                sent(there, maybe_here)
            returned(*pair, g).wait_recv()
        for part in range(parts):
            to_west(part, g).wait_send()
            to_east(part, g).wait_send()
        return carry

    lax.fori_loop(0, groups, finish, 0)


def body(tracers, fluxes, rate_coeff, first_reactant, second_reactant, product_species):
    parts = lax.axis_size("tracer")
    count, columns, length = tracers.shape
    total = length // GROUP
    groups = total // (2 * parts)
    species = parts * count
    reactions = rate_coeff.shape[0]

    def by_block(values):
        lead = values.shape[0]
        blocks = values.shape[2] // LANES
        return (
            values.reshape(lead, columns, blocks, LANES)
            .transpose(0, 2, 1, 3)
            .reshape(lead, blocks // BLOCKS, BLOCKS, columns, LANES)
        )

    natural = by_block(tracers)
    smem = pl.BlockSpec(memory_space=pltpu.SMEM)
    vmem = pl.BlockSpec(memory_space=pltpu.VMEM)
    anywhere = pl.BlockSpec(memory_space=pl.ANY)
    tile = (BLOCKS, columns, LANES)
    f32 = jnp.float32
    dma = pltpu.SemaphoreType.DMA
    coefs = (SIDES * columns + 2) * BLOCKS * 5
    out = pl.pallas_call(
        functools.partial(kernel, parts, count, groups),
        out_shape=jax.ShapeDtypeStruct(natural.shape, f32),
        in_specs=[smem] * 3 + [vmem] * 3 + [anywhere] * 2,
        out_specs=anywhere,
        scratch_shapes=[pltpu.VMEM((parts, SIDES, groups, count, *tile), f32)] * 2
        + [pltpu.VMEM((parts, groups, count, *tile), f32)] * 2
        + [pltpu.VMEM((SIDES, 2, groups, *tile), f32)]
        + [pltpu.VMEM((2, groups, *tile), f32)] * 2
        + [
            pltpu.VMEM((coefs, -(-groups // 8) * 8, LANES), f32),
            pltpu.VMEM((coefs, 8, LANES), f32),
            pltpu.VMEM((species * PITCH + 8, LANES), f32),
            pltpu.VMEM((reactions * PITCH + 8, LANES), f32),
            pltpu.VMEM((reactions, LANES), f32),
            pltpu.VMEM((species, reactions), jnp.bfloat16),
            pltpu.SMEM((reactions,), jnp.int32),
            pltpu.SMEM((reactions,), jnp.int32),
        ]
        + [dma((parts, 2, groups))] * 4
        + [dma((parts, groups))] * 4
        + [dma((2,))] * 4,
        compiler_params=pltpu.CompilerParams(
            vmem_limit_bytes=56 * 1024 * 1024, collective_id=0, has_side_effects=True
        ),
        name="belt",
    )(
        first_reactant,
        second_reactant,
        rate_coeff,
        first_reactant[None, :],
        second_reactant[None, :],
        product_species[None, :],
        by_block(fluxes),
        natural,
    )
    return (
        out.reshape(count, total * BLOCKS, columns, LANES).transpose(0, 2, 1, 3).reshape(tracers.shape)
    )


def solution(mesh):
    in_specs = (P("tracer", "region", None), P(None, "region", "tracer"), P(), P(), P(), P())
    out_specs = P("tracer", "region", None)
    return jax.shard_map(body, mesh=mesh, in_specs=in_specs, out_specs=out_specs, check_vma=False)
```

```python
import functools

import jax
import jax.numpy as jnp
from jax import lax
from jax.experimental import pallas as pl
from jax.experimental.pallas import tpu as pltpu
from jax.sharding import PartitionSpec as P

NY = 48
SUBSTEPS = 4
LANES = 128
BLOCKS = 3
COLUMNS = 2
ROWS = COLUMNS * BLOCKS
GROUP = BLOCKS * LANES
SIDES = 2
STRIP = SIDES * ROWS
PITCH = STRIP + 1
UNROLL = 32
MESH = pl.DeviceIdType.MESH


def south_of(values, lane):
    shifted = []
    for t in range(BLOCKS):
        source = values[t] if t == 0 else jnp.where(lane == LANES - 1, values[t - 1], values[t])
        shifted.append(pltpu.roll(source, 1, 1))
    return shifted


def north_of(values, lane):
    shifted = []
    for t in range(BLOCKS):
        last = t == BLOCKS - 1
        source = values[t] if last else jnp.where(lane == 0, values[t + 1], values[t])
        shifted.append(pltpu.roll(source, LANES - 1, 1))
    return shifted


def up(values):
    return jnp.maximum(values, 0.0)


def down(values):
    return jnp.minimum(values, 0.0)


def write_coefficients(groups, coef_ref, own_ref, west_ref, east_ref):
    lane = lax.broadcasted_iota(jnp.int32, (groups, LANES), 1)

    def read(ref, axis, column):
        rows = ref.reshape(2 * groups * ROWS, LANES)
        return [
            rows[pl.ds(axis * groups * ROWS + t * COLUMNS + column, groups, stride=ROWS), :]
            for t in range(BLOCKS)
        ]

    sources = [(west_ref, COLUMNS - 1)]
    sources += [(own_ref.at[side], column) for side in range(SIDES) for column in range(COLUMNS)]
    sources += [(east_ref, 0), (east_ref, 1)]
    u = [read(ref, 0, column) for ref, column in sources]
    for at in range(len(sources) - 1):
        v = read(sources[at][0], 1, sources[at][1])
        above = north_of(v, lane)
        for t in range(BLOCKS):
            y = (lane + t * LANES) % NY
            bottom, top = y == 0, y == NY - 1
            west_face, east_face = u[at][t], u[at + 1][t]
            center = (
                1.0
                + down(west_face)
                - up(east_face)
                + jnp.where(bottom, 0.0, down(v[t]))
                - jnp.where(top, 0.0, up(above[t]))
            )
            south = jnp.where(bottom, 0.0, up(v[t]))
            north = jnp.where(top, 0.0, -down(above[t]))
            for m, value in enumerate((center, up(west_face), -down(east_face), south, north)):
                coef_ref[(at * BLOCKS + t) * 5 + m, pl.ds(0, groups), :] = value


def kernel(
    parts,
    count,
    groups,
    first_ref,
    second_ref,
    rate_ref,
    first_row,
    second_row,
    product_row,
    flux_ref,
    nat_ref,
    out_ref,
    own_ref,
    stage_ref,
    west_ref,
    east_ref,
    flux_own,
    flux_west,
    flux_east,
    coef_ref,
    now_ref,
    c_ref,
    w_ref,
    k_ref,
    table_ref,
    first_at,
    second_at,
    g_send,
    g_recv,
    r_send,
    r_recv,
    w_send,
    w_recv,
    e_send,
    e_recv,
    f_send,
    f_recv,
    fh_send,
    fh_recv,
):
    region, me = lax.axis_index("region"), lax.axis_index("tracer")
    strips = lax.axis_size("region") // SIDES
    quad, bit, side = region // 4, (region // 2) % 2, region % 2
    strip = quad * 2 + side
    home = side == bit
    reactions = first_ref.shape[0]
    species = parts * count
    rows = count * ROWS

    def seat(at, b):
        return (at // 2) * 4 + b * 2 + at % 2

    west, east = seat((strip + strips - 1) % strips, bit), seat((strip + 1) % strips, bit)
    outer = jnp.where(side == 0, west, east)

    barrier = pltpu.get_barrier_semaphore()
    for shift in range(parts):
        for d in range(2):
            for e in range(2):
                if shift or d or e:
                    pl.semaphore_signal(
                        barrier,
                        1,
                        device_id=(quad * 4 + (bit + d) % 2 * 2 + (side + e) % 2, (me + shift) % parts),
                        device_id_type=MESH,
                    )
    pl.semaphore_signal(barrier, 1, device_id=(outer, me), device_id_type=MESH)
    pl.semaphore_wait(barrier, 4 * parts)

    def remote(source, target, send, recv, device):
        return pltpu.make_async_remote_copy(
            src_ref=source,
            dst_ref=target,
            send_sem=send,
            recv_sem=recv,
            device_id=device,
            device_id_type=MESH,
        )

    def start(copy_here, copy_there, maybe_here):
        if maybe_here:

            @pl.when(home)
            def _():
                copy_here().start()

            @pl.when(jnp.logical_not(home))
            def _():
                copy_there().start()

        else:
            copy_there().start()

    def sent(copy_there, maybe_here):
        if maybe_here:

            @pl.when(jnp.logical_not(home))
            def _():
                copy_there().wait_send()

        else:
            copy_there().wait_send()

    def gather(shift, d, g):
        owner, half = (me + shift) % parts, (bit + d) % 2
        source = nat_ref.at[:, (owner * 2 + half) * groups + g]
        target, arrived = own_ref.at[me, side, g], g_recv.at[me, side, g]
        return (
            lambda: pltpu.make_async_copy(source, target, arrived),
            lambda: remote(source, target, g_send.at[shift, d, g], arrived, (seat(quad * 2 + bit, half), owner)),
            shift == 0 and d == 0,
        )

    def gathered(part, s, g):
        return remote(
            own_ref.at[part, s, g], own_ref.at[part, s, g], g_send.at[0, 0, g], g_recv.at[part, s, g], (east, me)
        )

    def to_west(part, g):
        return remote(
            own_ref.at[part, 0, g], east_ref.at[part, g], e_send.at[part, g], e_recv.at[part, g], (west, me)
        )

    def to_east(part, g):
        return remote(
            own_ref.at[part, 1, g], west_ref.at[part, g], w_send.at[part, g], w_recv.at[part, g], (east, me)
        )

    def give_back(shift, e, g):
        part, s = (me + parts - shift) % parts, (side + e) % 2
        source, target = stage_ref.at[part, s, g], out_ref.at[:, (me * 2 + bit) * groups + g]
        arrived = r_recv.at[shift, (bit + side) % 2, g]
        return (
            lambda: pltpu.make_async_copy(source, target, arrived),
            lambda: remote(source, target, r_send.at[shift, e, g], arrived, (quad * 4 + side * 2 + s, part)),
            shift == 0 and e == 0,
        )

    def returned(shift, d, g):
        target = out_ref.at[:, g]
        return remote(stage_ref.at[0, 0, g], target, r_send.at[0, 0, g], r_recv.at[shift, d, g], (east, me))

    pairs = [(shift, d) for shift in (*range(1, parts), 0) for d in (1, 0)]

    def flux_gather(d):
        half = (bit + d) % 2
        source = flux_ref.at[:, pl.ds(half * groups, groups)]
        target, arrived = flux_own.at[side], f_recv.at[side]
        return (
            lambda: pltpu.make_async_copy(source, target, arrived),
            lambda: remote(source, target, f_send.at[d], arrived, (seat(quad * 2 + bit, half), me)),
            d == 0,
        )

    def flux_gathered(s):
        return remote(flux_own.at[s], flux_own.at[s], f_send.at[0], f_recv.at[s], (east, me))

    def flux_halo():
        return (
            remote(flux_own.at[0], flux_east, fh_send.at[0], fh_recv.at[0], (west, me)),
            remote(flux_own.at[1], flux_west, fh_send.at[1], fh_recv.at[1], (east, me)),
        )

    def pass_on(g):
        for shift in range(parts):
            part = (me + shift) % parts
            for s, onward in ((0, to_west), (1, to_east)):
                gathered(part, s, g).wait_recv()
                onward(part, g).start()

    for d in (1, 0):
        start(*flux_gather(d))
    straight = [pair for pair in pairs if pair[0] and not pair[1]]
    far = [pair for pair in pairs if pair[0] and pair[1]]
    for g in range(groups):

        @pl.when(side == 0)
        def _(g=g):
            for pair in far + straight:
                start(*gather(*pair, g))

        @pl.when(side != 0)
        def _(g=g):
            for pair in straight + far:
                start(*gather(*pair, g))

        for pair in pairs:
            if pair not in far and pair not in straight:
                start(*gather(*pair, g))

    def prepare(r, carry):
        first_at[r] = first_ref[r] * PITCH
        second_at[r] = second_ref[r] * PITCH
        k_ref[pl.ds(r, 1), :] = jnp.full((1, LANES), rate_ref[r], jnp.float32)
        return carry

    lax.fori_loop(0, reactions, prepare, 0)

    def build(i, carry):
        at = pl.multiple_of(i * 16, 16)
        order = lax.broadcasted_iota(jnp.int32, (16, reactions), 0) + at
        table_ref[pl.ds(at, 16), :] = (
            (product_row[...] == order).astype(jnp.float32)
            - (first_row[...] == order).astype(jnp.float32)
            - (second_row[...] == order).astype(jnp.float32)
        ).astype(jnp.bfloat16)
        return carry

    lax.fori_loop(0, species // 16, build, 0)

    for s in range(SIDES):
        flux_gathered(s).wait_recv()
    for copy in flux_halo():
        copy.start()
    for copy in flux_halo():
        copy.wait()
    for d in (1, 0):
        _, there, maybe_here = flux_gather(d)
        sent(there, maybe_here)
    write_coefficients(groups, coef_ref, flux_own, flux_west, flux_east)
    pass_on(0)

    lane = lax.broadcasted_iota(jnp.int32, (8, LANES), 1)
    batch = max(b for b in (1, 2, 4) if count % (8 * b) == 0)

    def one_group(g, carry):
        def spread(i, carry):
            now_ref[i, :, :] = coef_ref[i, pl.ds(g, 8, stride=0), :]
            return carry

        lax.fori_loop(0, coef_ref.shape[0], spread, 0)
        for part in range(parts):
            to_west(part, g).wait_recv()
            to_east(part, g).wait_recv()

        def step(cols, at, shifted):
            south, north = shifted
            return [
                now_ref[(at * BLOCKS + t) * 5, :, :] * cols[1][t]
                + now_ref[(at * BLOCKS + t) * 5 + 1, :, :] * cols[0][t]
                + now_ref[(at * BLOCKS + t) * 5 + 2, :, :] * cols[2][t]
                + now_ref[(at * BLOCKS + t) * 5 + 3, :, :] * south[t]
                + now_ref[(at * BLOCKS + t) * 5 + 4, :, :] * north[t]
                for t in range(BLOCKS)
            ]

        width = SIDES * COLUMNS
        for part in range(parts):
            slabs = [west_ref.at[part, g]]
            slabs += [own_ref.at[part, s, g] for s in range(SIDES)]
            slabs += [east_ref.at[part, g]]

            def advect(i, carry, part=part, slabs=slabs):
                def read(slab, column, block):
                    flat = slab.reshape(rows, LANES)
                    return [
                        flat[pl.ds(block * (8 * ROWS) + t * COLUMNS + column, 8, stride=ROWS), :]
                        for t in range(BLOCKS)
                    ]

                def shifts(values):
                    return south_of(values, lane), north_of(values, lane)

                blocks = [i * batch + j for j in range(batch)]
                cols = [
                    [read(slab, column, block) for slab in slabs for column in range(COLUMNS)]
                    for block in blocks
                ]
                moved = [[shifts(c[at + 1]) for at in range(width + 2)] for c in cols]
                mid = [
                    [step(c[at : at + 3], at, m[at]) for at in range(width + 2)]
                    for c, m in zip(cols, moved)
                ]
                moved = [[shifts(c[at + 1]) for at in range(width)] for c in mid]
                for block, c, m in zip(blocks, mid, moved):
                    for at in range(width):
                        new = step(c[at : at + 3], at + 1, m[at])
                        for t in range(BLOCKS):
                            place = at // COLUMNS * ROWS + t * COLUMNS + at % COLUMNS
                            begin = (part * count + block * 8) * PITCH + place
                            c_ref[pl.ds(begin, 8, stride=PITCH), :] = new[t]
                return carry

            lax.fori_loop(0, count // (8 * batch), advect, 0)

        @pl.when(g + 1 < groups)
        def _():
            pass_on(g + 1)

        def react(repeat, carry):
            def velocities(i, carry):
                for j in range(UNROLL):
                    r = i * UNROLL + j
                    one, two = first_at[r], second_at[r]
                    for at in (0, STRIP - 8):
                        w_ref[pl.ds(r * PITCH + at, 8), :] = (
                            c_ref[pl.ds(one + at, 8), :] * c_ref[pl.ds(two + at, 8), :]
                        )
                return carry

            lax.fori_loop(0, reactions // UNROLL, velocities, 0)

            for k in range(STRIP):
                w = w_ref[pl.ds(k, reactions, stride=PITCH), :] * k_ref[...]
                high = w.astype(jnp.bfloat16)
                low = (w - high.astype(jnp.float32)).astype(jnp.bfloat16)
                change = jnp.dot(
                    table_ref[...],
                    jnp.concatenate([high, low], axis=1),
                    preferred_element_type=jnp.float32,
                )
                where = pl.ds(k, species, stride=PITCH)
                c_ref[where, :] = c_ref[where, :] + (change[:, :LANES] + change[:, LANES:])
            return carry

        lax.fori_loop(0, SUBSTEPS, react, 0)

        for part in range(parts):

            def put(i, carry, part=part):
                for s in range(SIDES):
                    flat = stage_ref.at[part, s, g].reshape(rows, LANES)
                    for k in range(ROWS):
                        begin = (part * count + i * 8) * PITCH + s * ROWS + k
                        flat[pl.ds(i * (8 * ROWS) + k, 8, stride=ROWS), :] = c_ref[
                            pl.ds(begin, 8, stride=PITCH), :
                        ]
                return carry

            lax.fori_loop(0, count // 8, put, 0)
        for pair in pairs:
            start(*give_back(*pair, g))
        return carry

    lax.fori_loop(0, groups, one_group, 0)

    def finish(g, carry):
        for pair in pairs:
            for _, there, maybe_here in (gather(*pair, g), give_back(*pair, g)):
                sent(there, maybe_here)
            returned(*pair, g).wait_recv()
        for part in range(parts):
            to_west(part, g).wait_send()
            to_east(part, g).wait_send()
        return carry

    lax.fori_loop(0, groups, finish, 0)


def body(tracers, fluxes, rate_coeff, first_reactant, second_reactant, product_species):
    parts = lax.axis_size("tracer")
    count, columns, length = tracers.shape
    total = length // GROUP
    groups = total // (2 * parts)
    species = parts * count
    reactions = rate_coeff.shape[0]

    def by_block(values):
        lead = values.shape[0]
        blocks = values.shape[2] // LANES
        return (
            values.reshape(lead, columns, blocks, LANES)
            .transpose(0, 2, 1, 3)
            .reshape(lead, blocks // BLOCKS, BLOCKS, columns, LANES)
        )

    natural = by_block(tracers)
    smem = pl.BlockSpec(memory_space=pltpu.SMEM)
    vmem = pl.BlockSpec(memory_space=pltpu.VMEM)
    anywhere = pl.BlockSpec(memory_space=pl.ANY)
    tile = (BLOCKS, columns, LANES)
    f32 = jnp.float32
    dma = pltpu.SemaphoreType.DMA
    coefs = (SIDES * columns + 2) * BLOCKS * 5
    out = pl.pallas_call(
        functools.partial(kernel, parts, count, groups),
        out_shape=jax.ShapeDtypeStruct(natural.shape, f32),
        in_specs=[smem] * 3 + [vmem] * 3 + [anywhere] * 2,
        out_specs=vmem,
        scratch_shapes=[pltpu.VMEM((parts, SIDES, groups, count, *tile), f32)] * 2
        + [pltpu.VMEM((parts, groups, count, *tile), f32)] * 2
        + [pltpu.VMEM((SIDES, 2, groups, *tile), f32)]
        + [pltpu.VMEM((2, groups, *tile), f32)] * 2
        + [
            pltpu.VMEM((coefs, -(-groups // 8) * 8, LANES), f32),
            pltpu.VMEM((coefs, 8, LANES), f32),
            pltpu.VMEM((species * PITCH + 8, LANES), f32),
            pltpu.VMEM((reactions * PITCH + 8, LANES), f32),
            pltpu.VMEM((reactions, LANES), f32),
            pltpu.VMEM((species, reactions), jnp.bfloat16),
            pltpu.SMEM((reactions,), jnp.int32),
            pltpu.SMEM((reactions,), jnp.int32),
        ]
        + [dma((parts, 2, groups))] * 4
        + [dma((parts, groups))] * 4
        + [dma((2,))] * 4,
        compiler_params=pltpu.CompilerParams(
            vmem_limit_bytes=45 * 1024 * 1024, collective_id=0, has_side_effects=True
        ),
        name="belt",
    )(
        *[
            pltpu.with_memory_space_constraint(x, pltpu.HBM)
            for x in (
                first_reactant,
                second_reactant,
                rate_coeff,
                first_reactant[None, :],
                second_reactant[None, :],
                product_species[None, :],
                by_block(fluxes),
                natural,
            )
        ]
    )
    return (
        out.reshape(count, total * BLOCKS, columns, LANES).transpose(0, 2, 1, 3).reshape(tracers.shape)
    )


def solution(mesh):
    in_specs = (P("tracer", "region", None), P(None, "region", "tracer"), P(), P(), P(), P())
    out_specs = P("tracer", "region", None)
    return jax.shard_map(body, mesh=mesh, in_specs=in_specs, out_specs=out_specs, check_vma=False)
```

```python
import functools

import jax
import jax.numpy as jnp
from jax import lax
from jax.experimental import pallas as pl
from jax.experimental.pallas import tpu as pltpu
from jax.sharding import PartitionSpec as P

NY = 48
SUBSTEPS = 4
LANES = 128
BLOCKS = 3
COLUMNS = 2
ROWS = COLUMNS * BLOCKS
GROUP = BLOCKS * LANES
SIDES = 2
STRIP = SIDES * ROWS
PITCH = STRIP + 1
UNROLL = 32
MESH = pl.DeviceIdType.MESH


def south_of(values, lane):
    shifted = []
    for t in range(BLOCKS):
        source = values[t] if t == 0 else jnp.where(lane == LANES - 1, values[t - 1], values[t])
        shifted.append(pltpu.roll(source, 1, 1))
    return shifted


def north_of(values, lane):
    shifted = []
    for t in range(BLOCKS):
        last = t == BLOCKS - 1
        source = values[t] if last else jnp.where(lane == 0, values[t + 1], values[t])
        shifted.append(pltpu.roll(source, LANES - 1, 1))
    return shifted


def up(values):
    return jnp.maximum(values, 0.0)


def down(values):
    return jnp.minimum(values, 0.0)


def write_coefficients(groups, coef_ref, own_ref, west_ref, east_ref):
    lane = lax.broadcasted_iota(jnp.int32, (groups, LANES), 1)

    def read(ref, axis, column):
        rows = ref.reshape(2 * groups * ROWS, LANES)
        return [
            rows[pl.ds(axis * groups * ROWS + t * COLUMNS + column, groups, stride=ROWS), :]
            for t in range(BLOCKS)
        ]

    sources = [(west_ref, COLUMNS - 1)]
    sources += [(own_ref.at[side], column) for side in range(SIDES) for column in range(COLUMNS)]
    sources += [(east_ref, 0), (east_ref, 1)]
    u = [read(ref, 0, column) for ref, column in sources]
    for at in range(len(sources) - 1):
        v = read(sources[at][0], 1, sources[at][1])
        above = north_of(v, lane)
        for t in range(BLOCKS):
            y = (lane + t * LANES) % NY
            bottom, top = y == 0, y == NY - 1
            west_face, east_face = u[at][t], u[at + 1][t]
            center = (
                1.0
                + down(west_face)
                - up(east_face)
                + jnp.where(bottom, 0.0, down(v[t]))
                - jnp.where(top, 0.0, up(above[t]))
            )
            south = jnp.where(bottom, 0.0, up(v[t]))
            north = jnp.where(top, 0.0, -down(above[t]))
            for m, value in enumerate((center, up(west_face), -down(east_face), south, north)):
                coef_ref[(at * BLOCKS + t) * 5 + m, pl.ds(0, groups), :] = value


def kernel(
    parts,
    count,
    groups,
    first_ref,
    second_ref,
    rate_ref,
    first_row,
    second_row,
    product_row,
    flux_ref,
    nat_ref,
    out_ref,
    own_ref,
    stage_ref,
    west_ref,
    east_ref,
    flux_own,
    flux_west,
    flux_east,
    coef_ref,
    now_ref,
    c_ref,
    w_ref,
    k_ref,
    table_ref,
    first_at,
    second_at,
    g_send,
    g_recv,
    r_send,
    r_recv,
    w_send,
    w_recv,
    e_send,
    e_recv,
    f_send,
    f_recv,
    fh_send,
    fh_recv,
):
    region, me = lax.axis_index("region"), lax.axis_index("tracer")
    strips = lax.axis_size("region") // SIDES
    quad, bit, side = region // 4, (region // 2) % 2, region % 2
    strip = quad * 2 + side
    home = side == bit
    reactions = first_ref.shape[0]
    species = parts * count
    rows = count * ROWS

    def seat(at, b):
        return (at // 2) * 4 + b * 2 + at % 2

    west, east = seat((strip + strips - 1) % strips, bit), seat((strip + 1) % strips, bit)
    outer = jnp.where(side == 0, west, east)

    barrier = pltpu.get_barrier_semaphore()
    for shift in range(parts):
        for d in range(2):
            for e in range(2):
                if shift or d or e:
                    pl.semaphore_signal(
                        barrier,
                        1,
                        device_id=(quad * 4 + (bit + d) % 2 * 2 + (side + e) % 2, (me + shift) % parts),
                        device_id_type=MESH,
                    )
    pl.semaphore_signal(barrier, 1, device_id=(outer, me), device_id_type=MESH)
    pl.semaphore_wait(barrier, 4 * parts)

    def remote(source, target, send, recv, device):
        return pltpu.make_async_remote_copy(
            src_ref=source,
            dst_ref=target,
            send_sem=send,
            recv_sem=recv,
            device_id=device,
            device_id_type=MESH,
        )

    def start(copy_here, copy_there, maybe_here):
        if maybe_here:

            @pl.when(home)
            def _():
                copy_here().start()

            @pl.when(jnp.logical_not(home))
            def _():
                copy_there().start()

        else:
            copy_there().start()

    def sent(copy_there, maybe_here):
        if maybe_here:

            @pl.when(jnp.logical_not(home))
            def _():
                copy_there().wait_send()

        else:
            copy_there().wait_send()

    def gather(shift, d, g):
        owner, half = (me + shift) % parts, (bit + d) % 2
        source = nat_ref.at[:, (owner * 2 + half) * groups + g]
        target, arrived = own_ref.at[me, side, g], g_recv.at[me, side, g]
        return (
            lambda: pltpu.make_async_copy(source, target, arrived),
            lambda: remote(source, target, g_send.at[shift, d, g], arrived, (seat(quad * 2 + bit, half), owner)),
            shift == 0 and d == 0,
        )

    def gathered(part, s, g):
        return remote(
            own_ref.at[part, s, g], own_ref.at[part, s, g], g_send.at[0, 0, g], g_recv.at[part, s, g], (east, me)
        )

    def to_west(part, g):
        return remote(
            own_ref.at[part, 0, g], east_ref.at[part, g], e_send.at[part, g], e_recv.at[part, g], (west, me)
        )

    def to_east(part, g):
        return remote(
            own_ref.at[part, 1, g], west_ref.at[part, g], w_send.at[part, g], w_recv.at[part, g], (east, me)
        )

    def give_back(shift, e, g):
        part, s = (me + parts - shift) % parts, (side + e) % 2
        source, target = stage_ref.at[part, s, g], out_ref.at[:, (me * 2 + bit) * groups + g]
        arrived = r_recv.at[shift, (bit + side) % 2, g]
        return (
            lambda: pltpu.make_async_copy(source, target, arrived),
            lambda: remote(source, target, r_send.at[shift, e, g], arrived, (quad * 4 + side * 2 + s, part)),
            shift == 0 and e == 0,
        )

    def returned(shift, d, g):
        target = out_ref.at[:, g]
        return remote(stage_ref.at[0, 0, g], target, r_send.at[0, 0, g], r_recv.at[shift, d, g], (east, me))

    pairs = [(shift, d) for shift in (*range(1, parts), 0) for d in (1, 0)]

    def flux_gather(d):
        half = (bit + d) % 2
        source = flux_ref.at[:, pl.ds(half * groups, groups)]
        target, arrived = flux_own.at[side], f_recv.at[side]
        return (
            lambda: pltpu.make_async_copy(source, target, arrived),
            lambda: remote(source, target, f_send.at[d], arrived, (seat(quad * 2 + bit, half), me)),
            d == 0,
        )

    def flux_gathered(s):
        return remote(flux_own.at[s], flux_own.at[s], f_send.at[0], f_recv.at[s], (east, me))

    def flux_halo():
        return (
            remote(flux_own.at[0], flux_east, fh_send.at[0], fh_recv.at[0], (west, me)),
            remote(flux_own.at[1], flux_west, fh_send.at[1], fh_recv.at[1], (east, me)),
        )

    def pass_on(g, shifts):
        for shift in shifts:
            part = (me + shift + jnp.where(home, 0, 1)) % parts
            for s, onward in ((0, to_west), (1, to_east)):
                gathered(part, s, g).wait_recv()
                onward(part, g).start()

    for d in (1, 0):
        start(*flux_gather(d))
    straight = [pair for pair in pairs if pair[0] and not pair[1]]
    far = [pair for pair in pairs if pair[0] and pair[1]]
    for g in range(groups):

        @pl.when(side == 0)
        def _(g=g):
            for pair in far + straight:
                start(*gather(*pair, g))

        @pl.when(side != 0)
        def _(g=g):
            for pair in straight + far:
                start(*gather(*pair, g))

        for pair in pairs:
            if pair not in far and pair not in straight:
                start(*gather(*pair, g))

    def prepare(r, carry):
        first_at[r] = first_ref[r] * PITCH
        second_at[r] = second_ref[r] * PITCH
        k_ref[pl.ds(r, 1), :] = jnp.full((1, LANES), rate_ref[r], jnp.float32)
        return carry

    lax.fori_loop(0, reactions, prepare, 0)

    def build(i, carry):
        at = pl.multiple_of(i * 16, 16)
        order = lax.broadcasted_iota(jnp.int32, (16, reactions), 0) + at
        table_ref[pl.ds(at, 16), :] = (
            (product_row[...] == order).astype(jnp.float32)
            - (first_row[...] == order).astype(jnp.float32)
            - (second_row[...] == order).astype(jnp.float32)
        ).astype(jnp.bfloat16)
        return carry

    lax.fori_loop(0, species // 16, build, 0)

    for s in range(SIDES):
        flux_gathered(s).wait_recv()
    for copy in flux_halo():
        copy.start()
    for copy in flux_halo():
        copy.wait()
    for d in (1, 0):
        _, there, maybe_here = flux_gather(d)
        sent(there, maybe_here)
    write_coefficients(groups, coef_ref, flux_own, flux_west, flux_east)
    pass_on(0, range(parts))

    lane = lax.broadcasted_iota(jnp.int32, (8, LANES), 1)
    batch = max(b for b in (1, 2, 4) if count % (8 * b) == 0)

    def one_group(g, carry):
        def spread(i, carry):
            now_ref[i, :, :] = coef_ref[i, pl.ds(g, 8, stride=0), :]
            return carry

        lax.fori_loop(0, coef_ref.shape[0], spread, 0)
        def step(cols, at, shifted):
            south, north = shifted
            return [
                now_ref[(at * BLOCKS + t) * 5, :, :] * cols[1][t]
                + now_ref[(at * BLOCKS + t) * 5 + 1, :, :] * cols[0][t]
                + now_ref[(at * BLOCKS + t) * 5 + 2, :, :] * cols[2][t]
                + now_ref[(at * BLOCKS + t) * 5 + 3, :, :] * south[t]
                + now_ref[(at * BLOCKS + t) * 5 + 4, :, :] * north[t]
                for t in range(BLOCKS)
            ]

        width = SIDES * COLUMNS
        for shift in range(parts):
            part = (me + shift + jnp.where(home, 0, 1)) % parts
            to_west(part, g).wait_recv()
            to_east(part, g).wait_recv()
            slabs = [west_ref.at[part, g]]
            slabs += [own_ref.at[part, s, g] for s in range(SIDES)]
            slabs += [east_ref.at[part, g]]

            def advect(i, carry, part=part, slabs=slabs):
                def read(slab, column, block):
                    flat = slab.reshape(rows, LANES)
                    return [
                        flat[pl.ds(block * (8 * ROWS) + t * COLUMNS + column, 8, stride=ROWS), :]
                        for t in range(BLOCKS)
                    ]

                def shifts(values):
                    return south_of(values, lane), north_of(values, lane)

                blocks = [i * batch + j for j in range(batch)]
                cols = [
                    [read(slab, column, block) for slab in slabs for column in range(COLUMNS)]
                    for block in blocks
                ]
                moved = [[shifts(c[at + 1]) for at in range(width + 2)] for c in cols]
                mid = [
                    [step(c[at : at + 3], at, m[at]) for at in range(width + 2)]
                    for c, m in zip(cols, moved)
                ]
                moved = [[shifts(c[at + 1]) for at in range(width)] for c in mid]
                for block, c, m in zip(blocks, mid, moved):
                    for at in range(width):
                        new = step(c[at : at + 3], at + 1, m[at])
                        for t in range(BLOCKS):
                            place = at // COLUMNS * ROWS + t * COLUMNS + at % COLUMNS
                            begin = (part * count + block * 8) * PITCH + place
                            c_ref[pl.ds(begin, 8, stride=PITCH), :] = new[t]
                return carry

            lax.fori_loop(0, count // (8 * batch), advect, 0)

        @pl.when(g + 1 < groups)
        def _():
            pass_on(g + 1, range(parts - 1))

        def react(repeat, carry):
            def velocities(i, carry):
                for j in range(UNROLL):
                    r = i * UNROLL + j
                    one, two = first_at[r], second_at[r]
                    for at in (0, STRIP - 8):
                        w_ref[pl.ds(r * PITCH + at, 8), :] = (
                            c_ref[pl.ds(one + at, 8), :] * c_ref[pl.ds(two + at, 8), :]
                        )
                return carry

            lax.fori_loop(0, reactions // UNROLL, velocities, 0)

            for k in range(STRIP):
                w = w_ref[pl.ds(k, reactions, stride=PITCH), :] * k_ref[...]
                high = w.astype(jnp.bfloat16)
                low = (w - high.astype(jnp.float32)).astype(jnp.bfloat16)
                change = jnp.dot(
                    table_ref[...],
                    jnp.concatenate([high, low], axis=1),
                    preferred_element_type=jnp.float32,
                )
                where = pl.ds(k, species, stride=PITCH)
                c_ref[where, :] = c_ref[where, :] + (change[:, :LANES] + change[:, LANES:])

            @pl.when(jnp.logical_and(repeat == 0, g + 1 < groups))
            def _():
                pass_on(g + 1, range(parts - 1, parts))

            return carry

        lax.fori_loop(0, SUBSTEPS, react, 0)

        for part in range(parts):

            def put(i, carry, part=part):
                for s in range(SIDES):
                    flat = stage_ref.at[part, s, g].reshape(rows, LANES)
                    for k in range(ROWS):
                        begin = (part * count + i * 8) * PITCH + s * ROWS + k
                        flat[pl.ds(i * (8 * ROWS) + k, 8, stride=ROWS), :] = c_ref[
                            pl.ds(begin, 8, stride=PITCH), :
                        ]
                return carry

            lax.fori_loop(0, count // 8, put, 0)
        for pair in pairs:
            start(*give_back(*pair, g))
        return carry

    lax.fori_loop(0, groups, one_group, 0)

    def finish(g, carry):
        for pair in pairs:
            for _, there, maybe_here in (gather(*pair, g), give_back(*pair, g)):
                sent(there, maybe_here)
            returned(*pair, g).wait_recv()
        for part in range(parts):
            to_west(part, g).wait_send()
            to_east(part, g).wait_send()
        return carry

    lax.fori_loop(0, groups, finish, 0)


def body(tracers, fluxes, rate_coeff, first_reactant, second_reactant, product_species):
    parts = lax.axis_size("tracer")
    count, columns, length = tracers.shape
    total = length // GROUP
    groups = total // (2 * parts)
    species = parts * count
    reactions = rate_coeff.shape[0]

    def by_block(values):
        lead = values.shape[0]
        blocks = values.shape[2] // LANES
        return (
            values.reshape(lead, columns, blocks, LANES)
            .transpose(0, 2, 1, 3)
            .reshape(lead, blocks // BLOCKS, BLOCKS, columns, LANES)
        )

    natural = by_block(tracers)
    smem = pl.BlockSpec(memory_space=pltpu.SMEM)
    vmem = pl.BlockSpec(memory_space=pltpu.VMEM)
    anywhere = pl.BlockSpec(memory_space=pl.ANY)
    tile = (BLOCKS, columns, LANES)
    f32 = jnp.float32
    dma = pltpu.SemaphoreType.DMA
    coefs = (SIDES * columns + 2) * BLOCKS * 5
    out = pl.pallas_call(
        functools.partial(kernel, parts, count, groups),
        out_shape=jax.ShapeDtypeStruct(natural.shape, f32),
        in_specs=[smem] * 3 + [vmem] * 3 + [anywhere] * 2,
        out_specs=vmem,
        scratch_shapes=[pltpu.VMEM((parts, SIDES, groups, count, *tile), f32)] * 2
        + [pltpu.VMEM((parts, groups, count, *tile), f32)] * 2
        + [pltpu.VMEM((SIDES, 2, groups, *tile), f32)]
        + [pltpu.VMEM((2, groups, *tile), f32)] * 2
        + [
            pltpu.VMEM((coefs, -(-groups // 8) * 8, LANES), f32),
            pltpu.VMEM((coefs, 8, LANES), f32),
            pltpu.VMEM((species * PITCH + 8, LANES), f32),
            pltpu.VMEM((reactions * PITCH + 8, LANES), f32),
            pltpu.VMEM((reactions, LANES), f32),
            pltpu.VMEM((species, reactions), jnp.bfloat16),
            pltpu.SMEM((reactions,), jnp.int32),
            pltpu.SMEM((reactions,), jnp.int32),
        ]
        + [dma((parts, 2, groups))] * 4
        + [dma((parts, groups))] * 4
        + [dma((2,))] * 4,
        compiler_params=pltpu.CompilerParams(
            vmem_limit_bytes=45 * 1024 * 1024, collective_id=0, has_side_effects=True
        ),
        name="belt",
    )(
        *[
            pltpu.with_memory_space_constraint(x, pltpu.HBM)
            for x in (
                first_reactant,
                second_reactant,
                rate_coeff,
                first_reactant[None, :],
                second_reactant[None, :],
                product_species[None, :],
                by_block(fluxes),
                natural,
            )
        ]
    )
    return (
        out.reshape(count, total * BLOCKS, columns, LANES).transpose(0, 2, 1, 3).reshape(tracers.shape)
    )


def solution(mesh):
    in_specs = (P("tracer", "region", None), P(None, "region", "tracer"), P(), P(), P(), P())
    out_specs = P("tracer", "region", None)
    return jax.shard_map(body, mesh=mesh, in_specs=in_specs, out_specs=out_specs, check_vma=False)
```

```python
import functools

import jax
import jax.numpy as jnp
from jax import lax
from jax.experimental import pallas as pl
from jax.experimental.pallas import tpu as pltpu
from jax.sharding import PartitionSpec as P

NY = 48
SUBSTEPS = 4
LANES = 128
BLOCKS = 3
COLUMNS = 2
ROWS = COLUMNS * BLOCKS
GROUP = BLOCKS * LANES
SIDES = 2
STRIP = SIDES * ROWS
PITCH = STRIP + 1
UNROLL = 32
MESH = pl.DeviceIdType.MESH


def south_of(values, lane):
    shifted = []
    for t in range(BLOCKS):
        source = values[t] if t == 0 else jnp.where(lane == LANES - 1, values[t - 1], values[t])
        shifted.append(pltpu.roll(source, 1, 1))
    return shifted


def north_of(values, lane):
    shifted = []
    for t in range(BLOCKS):
        last = t == BLOCKS - 1
        source = values[t] if last else jnp.where(lane == 0, values[t + 1], values[t])
        shifted.append(pltpu.roll(source, LANES - 1, 1))
    return shifted


def up(values):
    return jnp.maximum(values, 0.0)


def down(values):
    return jnp.minimum(values, 0.0)


def write_coefficients(groups, coef_ref, own_ref, west_ref, east_ref):
    lane = lax.broadcasted_iota(jnp.int32, (groups, LANES), 1)

    def read(ref, axis, column):
        rows = ref.reshape(2 * groups * ROWS, LANES)
        return [
            rows[pl.ds(axis * groups * ROWS + t * COLUMNS + column, groups, stride=ROWS), :]
            for t in range(BLOCKS)
        ]

    sources = [(west_ref, COLUMNS - 1)]
    sources += [(own_ref.at[side], column) for side in range(SIDES) for column in range(COLUMNS)]
    sources += [(east_ref, 0), (east_ref, 1)]
    u = [read(ref, 0, column) for ref, column in sources]
    for at in range(len(sources) - 1):
        v = read(sources[at][0], 1, sources[at][1])
        above = north_of(v, lane)
        for t in range(BLOCKS):
            y = (lane + t * LANES) % NY
            bottom, top = y == 0, y == NY - 1
            west_face, east_face = u[at][t], u[at + 1][t]
            center = (
                1.0
                + down(west_face)
                - up(east_face)
                + jnp.where(bottom, 0.0, down(v[t]))
                - jnp.where(top, 0.0, up(above[t]))
            )
            south = jnp.where(bottom, 0.0, up(v[t]))
            north = jnp.where(top, 0.0, -down(above[t]))
            for m, value in enumerate((center, up(west_face), -down(east_face), south, north)):
                coef_ref[(at * BLOCKS + t) * 5 + m, pl.ds(0, groups), :] = value


def kernel(
    parts,
    count,
    groups,
    first_ref,
    second_ref,
    rate_ref,
    first_row,
    second_row,
    product_row,
    flux_ref,
    nat_ref,
    out_ref,
    own_ref,
    stage_ref,
    west_ref,
    east_ref,
    flux_own,
    flux_west,
    flux_east,
    coef_ref,
    now_ref,
    c_ref,
    w_ref,
    k_ref,
    table_ref,
    first_at,
    second_at,
    g_send,
    g_recv,
    r_send,
    r_recv,
    w_send,
    w_recv,
    e_send,
    e_recv,
    f_send,
    f_recv,
    fh_send,
    fh_recv,
):
    region, me = lax.axis_index("region"), lax.axis_index("tracer")
    strips = lax.axis_size("region") // SIDES
    quad, bit, side = region // 4, (region // 2) % 2, region % 2
    strip = quad * 2 + side
    home = side == bit
    reactions = first_ref.shape[0]
    species = parts * count
    rows = count * ROWS

    def seat(at, b):
        return (at // 2) * 4 + b * 2 + at % 2

    west, east = seat((strip + strips - 1) % strips, bit), seat((strip + 1) % strips, bit)
    outer = jnp.where(side == 0, west, east)

    barrier = pltpu.get_barrier_semaphore()
    for shift in range(parts):
        for d in range(2):
            for e in range(2):
                if shift or d or e:
                    pl.semaphore_signal(
                        barrier,
                        1,
                        device_id=(quad * 4 + (bit + d) % 2 * 2 + (side + e) % 2, (me + shift) % parts),
                        device_id_type=MESH,
                    )
    pl.semaphore_signal(barrier, 1, device_id=(outer, me), device_id_type=MESH)
    pl.semaphore_wait(barrier, 4 * parts)

    def remote(source, target, send, recv, device):
        return pltpu.make_async_remote_copy(
            src_ref=source,
            dst_ref=target,
            send_sem=send,
            recv_sem=recv,
            device_id=device,
            device_id_type=MESH,
        )

    def start(copy_here, copy_there, maybe_here):
        if maybe_here:

            @pl.when(home)
            def _():
                copy_here().start()

            @pl.when(jnp.logical_not(home))
            def _():
                copy_there().start()

        else:
            copy_there().start()

    def sent(copy_there, maybe_here):
        if maybe_here:

            @pl.when(jnp.logical_not(home))
            def _():
                copy_there().wait_send()

        else:
            copy_there().wait_send()

    def gather(shift, d, g):
        owner, half = (me + shift) % parts, (bit + d) % 2
        source = nat_ref.at[:, (owner * 2 + half) * groups + g]
        target, arrived = own_ref.at[me, side, g], g_recv.at[me, side, g]
        return (
            lambda: pltpu.make_async_copy(source, target, arrived),
            lambda: remote(source, target, g_send.at[shift, d, g], arrived, (seat(quad * 2 + bit, half), owner)),
            shift == 0 and d == 0,
        )

    def gathered(part, s, g):
        return remote(
            own_ref.at[part, s, g], own_ref.at[part, s, g], g_send.at[0, 0, g], g_recv.at[part, s, g], (east, me)
        )

    def to_west(part, g):
        return remote(
            own_ref.at[part, 0, g], east_ref.at[part, g], e_send.at[part, g], e_recv.at[part, g], (west, me)
        )

    def to_east(part, g):
        return remote(
            own_ref.at[part, 1, g], west_ref.at[part, g], w_send.at[part, g], w_recv.at[part, g], (east, me)
        )

    def give_back(shift, e, g):
        part, s = (me + parts - shift) % parts, (side + e) % 2
        source, target = stage_ref.at[part, s, g], out_ref.at[:, (me * 2 + bit) * groups + g]
        arrived = r_recv.at[shift, (bit + side) % 2, g]
        return (
            lambda: pltpu.make_async_copy(source, target, arrived),
            lambda: remote(source, target, r_send.at[shift, e, g], arrived, (quad * 4 + side * 2 + s, part)),
            shift == 0 and e == 0,
        )

    def returned(shift, d, g):
        target = out_ref.at[:, g]
        return remote(stage_ref.at[0, 0, g], target, r_send.at[0, 0, g], r_recv.at[shift, d, g], (east, me))

    pairs = [(shift, d) for shift in (*range(1, parts), 0) for d in (1, 0)]

    def flux_gather(d):
        half = (bit + d) % 2
        source = flux_ref.at[:, pl.ds(half * groups, groups)]
        target, arrived = flux_own.at[side], f_recv.at[side]
        return (
            lambda: pltpu.make_async_copy(source, target, arrived),
            lambda: remote(source, target, f_send.at[d], arrived, (seat(quad * 2 + bit, half), me)),
            d == 0,
        )

    def flux_gathered(s):
        return remote(flux_own.at[s], flux_own.at[s], f_send.at[0], f_recv.at[s], (east, me))

    def flux_halo():
        return (
            remote(flux_own.at[0], flux_east, fh_send.at[0], fh_recv.at[0], (west, me)),
            remote(flux_own.at[1], flux_west, fh_send.at[1], fh_recv.at[1], (east, me)),
        )

    def pass_on(g, shifts):
        for shift in shifts:
            part = (me + shift + jnp.where(home, 0, 1)) % parts
            for s, onward in ((0, to_west), (1, to_east)):
                gathered(part, s, g).wait_recv()
                onward(part, g).start()

    for d in (1, 0):
        start(*flux_gather(d))
    straight = [pair for pair in pairs if pair[0] and not pair[1]]
    far = [pair for pair in pairs if pair[0] and pair[1]]
    for g in range(groups):

        @pl.when(side == 0)
        def _(g=g):
            for pair in far + straight:
                start(*gather(*pair, g))

        @pl.when(side != 0)
        def _(g=g):
            for pair in straight + far:
                start(*gather(*pair, g))

        for pair in pairs:
            if pair not in far and pair not in straight:
                start(*gather(*pair, g))

    def prepare(r, carry):
        first_at[r] = first_ref[r] * PITCH
        second_at[r] = second_ref[r] * PITCH
        k_ref[pl.ds(r, 1), :] = jnp.full((1, LANES), rate_ref[r], jnp.float32)
        return carry

    lax.fori_loop(0, reactions, prepare, 0)

    def build(i, carry):
        at = pl.multiple_of(i * 16, 16)
        order = lax.broadcasted_iota(jnp.int32, (16, reactions), 0) + at
        table_ref[pl.ds(at, 16), :] = (
            (product_row[...] == order).astype(jnp.float32)
            - (first_row[...] == order).astype(jnp.float32)
            - (second_row[...] == order).astype(jnp.float32)
        ).astype(jnp.bfloat16)
        return carry

    lax.fori_loop(0, species // 16, build, 0)

    for s in range(SIDES):
        flux_gathered(s).wait_recv()
    for copy in flux_halo():
        copy.start()
    for copy in flux_halo():
        copy.wait()
    for d in (1, 0):
        _, there, maybe_here = flux_gather(d)
        sent(there, maybe_here)
    write_coefficients(groups, coef_ref, flux_own, flux_west, flux_east)
    pass_on(0, range(parts))

    lane = lax.broadcasted_iota(jnp.int32, (8, LANES), 1)
    batch = max(b for b in (1, 2, 4) if count % (8 * b) == 0)

    def one_group(g, carry):
        def spread(i, carry):
            now_ref[i, :, :] = coef_ref[i, pl.ds(g, 8, stride=0), :]
            return carry

        lax.fori_loop(0, coef_ref.shape[0], spread, 0)
        def step(cols, at, shifted):
            south, north = shifted
            return [
                now_ref[(at * BLOCKS + t) * 5, :, :] * cols[1][t]
                + now_ref[(at * BLOCKS + t) * 5 + 1, :, :] * cols[0][t]
                + now_ref[(at * BLOCKS + t) * 5 + 2, :, :] * cols[2][t]
                + now_ref[(at * BLOCKS + t) * 5 + 3, :, :] * south[t]
                + now_ref[(at * BLOCKS + t) * 5 + 4, :, :] * north[t]
                for t in range(BLOCKS)
            ]

        width = SIDES * COLUMNS
        for shift in range(parts):
            part = (me + shift + jnp.where(home, 0, 1)) % parts
            to_west(part, g).wait_recv()
            to_east(part, g).wait_recv()
            slabs = [west_ref.at[part, g]]
            slabs += [own_ref.at[part, s, g] for s in range(SIDES)]
            slabs += [east_ref.at[part, g]]

            def advect(i, carry, part=part, slabs=slabs):
                def read(slab, column, block):
                    flat = slab.reshape(rows, LANES)
                    return [
                        flat[pl.ds(block * (8 * ROWS) + t * COLUMNS + column, 8, stride=ROWS), :]
                        for t in range(BLOCKS)
                    ]

                def shifts(values):
                    return south_of(values, lane), north_of(values, lane)

                blocks = [i * batch + j for j in range(batch)]
                cols = [
                    [read(slab, column, block) for slab in slabs for column in range(COLUMNS)]
                    for block in blocks
                ]
                moved = [[shifts(c[at + 1]) for at in range(width + 2)] for c in cols]
                mid = [
                    [step(c[at : at + 3], at, m[at]) for at in range(width + 2)]
                    for c, m in zip(cols, moved)
                ]
                moved = [[shifts(c[at + 1]) for at in range(width)] for c in mid]
                for block, c, m in zip(blocks, mid, moved):
                    for at in range(width):
                        new = step(c[at : at + 3], at + 1, m[at])
                        for t in range(BLOCKS):
                            place = at // COLUMNS * ROWS + t * COLUMNS + at % COLUMNS
                            begin = (part * count + block * 8) * PITCH + place
                            c_ref[pl.ds(begin, 8, stride=PITCH), :] = new[t]
                return carry

            lax.fori_loop(0, count // (8 * batch), advect, 0)

        @pl.when(g + 1 < groups)
        def _():
            pass_on(g + 1, range(parts - 1))

        def react(repeat, carry):
            def velocities(i, carry):
                for j in range(UNROLL):
                    r = i * UNROLL + j
                    one, two = first_at[r], second_at[r]
                    for at in (0, STRIP - 8):
                        w_ref[pl.ds(r * PITCH + at, 8), :] = (
                            c_ref[pl.ds(one + at, 8), :] * c_ref[pl.ds(two + at, 8), :]
                        )
                return carry

            lax.fori_loop(0, reactions // UNROLL, velocities, 0)

            for k in range(STRIP):
                w = w_ref[pl.ds(k, reactions, stride=PITCH), :] * k_ref[...]
                high = w.astype(jnp.bfloat16)
                low = (w - high.astype(jnp.float32)).astype(jnp.bfloat16)
                change = jnp.dot(
                    table_ref[...],
                    jnp.concatenate([high, low], axis=1),
                    preferred_element_type=jnp.float32,
                )
                where = pl.ds(k, species, stride=PITCH)
                c_ref[where, :] = c_ref[where, :] + (change[:, :LANES] + change[:, LANES:])

            @pl.when(jnp.logical_and(repeat == 0, g + 1 < groups))
            def _():
                pass_on(g + 1, range(parts - 1, parts))

            return carry

        lax.fori_loop(0, SUBSTEPS, react, 0)

        for part in range(parts):

            def put(i, carry, part=part):
                for s in range(SIDES):
                    flat = stage_ref.at[part, s, g].reshape(rows, LANES)
                    for k in range(ROWS):
                        begin = (part * count + i * 8) * PITCH + s * ROWS + k
                        flat[pl.ds(i * (8 * ROWS) + k, 8, stride=ROWS), :] = c_ref[
                            pl.ds(begin, 8, stride=PITCH), :
                        ]
                return carry

            lax.fori_loop(0, count // 8, put, 0)
        for pair in reversed(pairs):
            start(*give_back(*pair, g))
        return carry

    lax.fori_loop(0, groups, one_group, 0)

    def finish(g, carry):
        for pair in pairs:
            for _, there, maybe_here in (gather(*pair, g), give_back(*pair, g)):
                sent(there, maybe_here)
            returned(*pair, g).wait_recv()
        for part in range(parts):
            to_west(part, g).wait_send()
            to_east(part, g).wait_send()
        return carry

    lax.fori_loop(0, groups, finish, 0)


def body(tracers, fluxes, rate_coeff, first_reactant, second_reactant, product_species):
    parts = lax.axis_size("tracer")
    count, columns, length = tracers.shape
    total = length // GROUP
    groups = total // (2 * parts)
    species = parts * count
    reactions = rate_coeff.shape[0]

    def by_block(values):
        lead = values.shape[0]
        blocks = values.shape[2] // LANES
        return (
            values.reshape(lead, columns, blocks, LANES)
            .transpose(0, 2, 1, 3)
            .reshape(lead, blocks // BLOCKS, BLOCKS, columns, LANES)
        )

    natural = by_block(tracers)
    smem = pl.BlockSpec(memory_space=pltpu.SMEM)
    vmem = pl.BlockSpec(memory_space=pltpu.VMEM)
    anywhere = pl.BlockSpec(memory_space=pl.ANY)
    tile = (BLOCKS, columns, LANES)
    f32 = jnp.float32
    dma = pltpu.SemaphoreType.DMA
    coefs = (SIDES * columns + 2) * BLOCKS * 5
    out = pl.pallas_call(
        functools.partial(kernel, parts, count, groups),
        out_shape=jax.ShapeDtypeStruct(natural.shape, f32),
        in_specs=[smem] * 3 + [vmem] * 3 + [anywhere] * 2,
        out_specs=vmem,
        scratch_shapes=[pltpu.VMEM((parts, SIDES, groups, count, *tile), f32)] * 2
        + [pltpu.VMEM((parts, groups, count, *tile), f32)] * 2
        + [pltpu.VMEM((SIDES, 2, groups, *tile), f32)]
        + [pltpu.VMEM((2, groups, *tile), f32)] * 2
        + [
            pltpu.VMEM((coefs, -(-groups // 8) * 8, LANES), f32),
            pltpu.VMEM((coefs, 8, LANES), f32),
            pltpu.VMEM((species * PITCH + 8, LANES), f32),
            pltpu.VMEM((reactions * PITCH + 8, LANES), f32),
            pltpu.VMEM((reactions, LANES), f32),
            pltpu.VMEM((species, reactions), jnp.bfloat16),
            pltpu.SMEM((reactions,), jnp.int32),
            pltpu.SMEM((reactions,), jnp.int32),
        ]
        + [dma((parts, 2, groups))] * 4
        + [dma((parts, groups))] * 4
        + [dma((2,))] * 4,
        compiler_params=pltpu.CompilerParams(
            vmem_limit_bytes=45 * 1024 * 1024, collective_id=0, has_side_effects=True
        ),
        name="belt",
    )(
        *[
            pltpu.with_memory_space_constraint(x, pltpu.HBM)
            for x in (
                first_reactant,
                second_reactant,
                rate_coeff,
                first_reactant[None, :],
                second_reactant[None, :],
                product_species[None, :],
                by_block(fluxes),
                natural,
            )
        ]
    )
    return (
        out.reshape(count, total * BLOCKS, columns, LANES).transpose(0, 2, 1, 3).reshape(tracers.shape)
    )


def solution(mesh):
    in_specs = (P("tracer", "region", None), P(None, "region", "tracer"), P(), P(), P(), P())
    out_specs = P("tracer", "region", None)
    return jax.shard_map(body, mesh=mesh, in_specs=in_specs, out_specs=out_specs, check_vma=False)
```

```python
import functools

import jax
import jax.numpy as jnp
from jax import lax
from jax.experimental import pallas as pl
from jax.experimental.pallas import tpu as pltpu
from jax.sharding import PartitionSpec as P

NY = 48
SUBSTEPS = 4
LANES = 128
BLOCKS = 3
COLUMNS = 2
ROWS = COLUMNS * BLOCKS
GROUP = BLOCKS * LANES
SIDES = 2
STRIP = SIDES * ROWS
PITCH = STRIP + 1
UNROLL = 32
MESH = pl.DeviceIdType.MESH


def south_of(values, lane):
    shifted = []
    for t in range(BLOCKS):
        source = values[t] if t == 0 else jnp.where(lane == LANES - 1, values[t - 1], values[t])
        shifted.append(pltpu.roll(source, 1, 1))
    return shifted


def north_of(values, lane):
    shifted = []
    for t in range(BLOCKS):
        last = t == BLOCKS - 1
        source = values[t] if last else jnp.where(lane == 0, values[t + 1], values[t])
        shifted.append(pltpu.roll(source, LANES - 1, 1))
    return shifted


def up(values):
    return jnp.maximum(values, 0.0)


def down(values):
    return jnp.minimum(values, 0.0)


def write_coefficients(groups, coef_ref, own_ref, west_ref, east_ref):
    lane = lax.broadcasted_iota(jnp.int32, (groups, LANES), 1)

    def read(ref, axis, column):
        rows = ref.reshape(2 * groups * ROWS, LANES)
        return [
            rows[pl.ds(axis * groups * ROWS + t * COLUMNS + column, groups, stride=ROWS), :]
            for t in range(BLOCKS)
        ]

    sources = [(west_ref, COLUMNS - 1)]
    sources += [(own_ref.at[side], column) for side in range(SIDES) for column in range(COLUMNS)]
    sources += [(east_ref, 0), (east_ref, 1)]
    u = [read(ref, 0, column) for ref, column in sources]
    for at in range(len(sources) - 1):
        v = read(sources[at][0], 1, sources[at][1])
        above = north_of(v, lane)
        for t in range(BLOCKS):
            y = (lane + t * LANES) % NY
            bottom, top = y == 0, y == NY - 1
            west_face, east_face = u[at][t], u[at + 1][t]
            center = (
                1.0
                + down(west_face)
                - up(east_face)
                + jnp.where(bottom, 0.0, down(v[t]))
                - jnp.where(top, 0.0, up(above[t]))
            )
            south = jnp.where(bottom, 0.0, up(v[t]))
            north = jnp.where(top, 0.0, -down(above[t]))
            for m, value in enumerate((center, up(west_face), -down(east_face), south, north)):
                coef_ref[(at * BLOCKS + t) * 5 + m, pl.ds(0, groups), :] = value


def kernel(
    parts,
    count,
    groups,
    first_ref,
    second_ref,
    rate_ref,
    first_row,
    second_row,
    product_row,
    flux_ref,
    nat_ref,
    out_ref,
    own_ref,
    stage_ref,
    west_ref,
    east_ref,
    flux_own,
    flux_west,
    flux_east,
    coef_ref,
    now_ref,
    c_ref,
    w_ref,
    k_ref,
    table_ref,
    first_at,
    second_at,
    g_send,
    g_recv,
    r_send,
    r_recv,
    w_send,
    w_recv,
    e_send,
    e_recv,
    f_send,
    f_recv,
    fh_send,
    fh_recv,
):
    region, me = lax.axis_index("region"), lax.axis_index("tracer")
    strips = lax.axis_size("region") // SIDES
    quad, bit, side = region // 4, (region // 2) % 2, region % 2
    strip = quad * 2 + side
    home = side == bit
    reactions = first_ref.shape[0]
    species = parts * count
    rows = count * ROWS

    def seat(at, b):
        return (at // 2) * 4 + b * 2 + at % 2

    west, east = seat((strip + strips - 1) % strips, bit), seat((strip + 1) % strips, bit)
    outer = jnp.where(side == 0, west, east)

    barrier = pltpu.get_barrier_semaphore()
    for shift in range(parts):
        for d in range(2):
            for e in range(2):
                if shift or d or e:
                    pl.semaphore_signal(
                        barrier,
                        1,
                        device_id=(quad * 4 + (bit + d) % 2 * 2 + (side + e) % 2, (me + shift) % parts),
                        device_id_type=MESH,
                    )
    pl.semaphore_signal(barrier, 1, device_id=(outer, me), device_id_type=MESH)
    pl.semaphore_wait(barrier, 4 * parts)

    def remote(source, target, send, recv, device):
        return pltpu.make_async_remote_copy(
            src_ref=source,
            dst_ref=target,
            send_sem=send,
            recv_sem=recv,
            device_id=device,
            device_id_type=MESH,
        )

    def start(copy_here, copy_there, maybe_here):
        if maybe_here:

            @pl.when(home)
            def _():
                copy_here().start()

            @pl.when(jnp.logical_not(home))
            def _():
                copy_there().start()

        else:
            copy_there().start()

    def sent(copy_there, maybe_here):
        if maybe_here:

            @pl.when(jnp.logical_not(home))
            def _():
                copy_there().wait_send()

        else:
            copy_there().wait_send()

    def gather(shift, d, g):
        owner, half = (me + shift) % parts, (bit + d) % 2
        source = nat_ref.at[:, (owner * 2 + half) * groups + g]
        target, arrived = own_ref.at[me, side, g], g_recv.at[me, side, g]
        return (
            lambda: pltpu.make_async_copy(source, target, arrived),
            lambda: remote(source, target, g_send.at[shift, d, g], arrived, (seat(quad * 2 + bit, half), owner)),
            shift == 0 and d == 0,
        )

    def gathered(part, s, g):
        return remote(
            own_ref.at[part, s, g], own_ref.at[part, s, g], g_send.at[0, 0, g], g_recv.at[part, s, g], (east, me)
        )

    def to_west(part, g):
        return remote(
            own_ref.at[part, 0, g], east_ref.at[part, g], e_send.at[part, g], e_recv.at[part, g], (west, me)
        )

    def to_east(part, g):
        return remote(
            own_ref.at[part, 1, g], west_ref.at[part, g], w_send.at[part, g], w_recv.at[part, g], (east, me)
        )

    def give_back(shift, e, g):
        part, s = (me + parts - shift) % parts, (side + e) % 2
        source, target = stage_ref.at[part, s, g], out_ref.at[:, (me * 2 + bit) * groups + g]
        arrived = r_recv.at[shift, (bit + side) % 2, g]
        return (
            lambda: pltpu.make_async_copy(source, target, arrived),
            lambda: remote(source, target, r_send.at[shift, e, g], arrived, (quad * 4 + side * 2 + s, part)),
            shift == 0 and e == 0,
        )

    def returned(shift, d, g):
        target = out_ref.at[:, g]
        return remote(stage_ref.at[0, 0, g], target, r_send.at[0, 0, g], r_recv.at[shift, d, g], (east, me))

    pairs = [(shift, d) for shift in (*range(1, parts), 0) for d in (1, 0)]

    def flux_gather(d):
        half = (bit + d) % 2
        source = flux_ref.at[:, pl.ds(half * groups, groups)]
        target, arrived = flux_own.at[side], f_recv.at[side]
        return (
            lambda: pltpu.make_async_copy(source, target, arrived),
            lambda: remote(source, target, f_send.at[d], arrived, (seat(quad * 2 + bit, half), me)),
            d == 0,
        )

    def flux_gathered(s):
        return remote(flux_own.at[s], flux_own.at[s], f_send.at[0], f_recv.at[s], (east, me))

    def flux_halo():
        return (
            remote(flux_own.at[0], flux_east, fh_send.at[0], fh_recv.at[0], (west, me)),
            remote(flux_own.at[1], flux_west, fh_send.at[1], fh_recv.at[1], (east, me)),
        )

    def pass_on(g, shifts):
        for shift in shifts:
            part = (me + shift + jnp.where(home, 0, 1)) % parts
            for s, onward in ((1, to_east), (0, to_west)):
                gathered(part, s, g).wait_recv()
                onward(part, g).start()

    for d in (1, 0):
        start(*flux_gather(d))
    straight = [pair for pair in pairs if pair[0] and not pair[1]]
    far = [pair for pair in pairs if pair[0] and pair[1]]
    for g in range(groups):

        @pl.when(side == 0)
        def _(g=g):
            for pair in far + straight:
                start(*gather(*pair, g))

        @pl.when(side != 0)
        def _(g=g):
            for pair in straight + far:
                start(*gather(*pair, g))

        for pair in pairs:
            if pair not in far and pair not in straight:
                start(*gather(*pair, g))

    def prepare(r, carry):
        first_at[r] = first_ref[r] * PITCH
        second_at[r] = second_ref[r] * PITCH
        k_ref[pl.ds(r, 1), :] = jnp.full((1, LANES), rate_ref[r], jnp.float32)
        return carry

    lax.fori_loop(0, reactions, prepare, 0)

    def build(i, carry):
        at = pl.multiple_of(i * 16, 16)
        order = lax.broadcasted_iota(jnp.int32, (16, reactions), 0) + at
        table_ref[pl.ds(at, 16), :] = (
            (product_row[...] == order).astype(jnp.float32)
            - (first_row[...] == order).astype(jnp.float32)
            - (second_row[...] == order).astype(jnp.float32)
        ).astype(jnp.bfloat16)
        return carry

    lax.fori_loop(0, species // 16, build, 0)

    for s in range(SIDES):
        flux_gathered(s).wait_recv()
    for copy in flux_halo():
        copy.start()
    for copy in flux_halo():
        copy.wait()
    for d in (1, 0):
        _, there, maybe_here = flux_gather(d)
        sent(there, maybe_here)
    write_coefficients(groups, coef_ref, flux_own, flux_west, flux_east)
    pass_on(0, range(parts))

    lane = lax.broadcasted_iota(jnp.int32, (8, LANES), 1)
    batch = max(b for b in (1, 2, 4) if count % (8 * b) == 0)

    def one_group(g, carry):
        def spread(i, carry):
            now_ref[i, :, :] = coef_ref[i, pl.ds(g, 8, stride=0), :]
            return carry

        lax.fori_loop(0, coef_ref.shape[0], spread, 0)
        def step(cols, at, shifted):
            south, north = shifted
            return [
                now_ref[(at * BLOCKS + t) * 5, :, :] * cols[1][t]
                + now_ref[(at * BLOCKS + t) * 5 + 1, :, :] * cols[0][t]
                + now_ref[(at * BLOCKS + t) * 5 + 2, :, :] * cols[2][t]
                + now_ref[(at * BLOCKS + t) * 5 + 3, :, :] * south[t]
                + now_ref[(at * BLOCKS + t) * 5 + 4, :, :] * north[t]
                for t in range(BLOCKS)
            ]

        width = SIDES * COLUMNS
        for shift in range(parts):
            part = (me + shift + jnp.where(home, 0, 1)) % parts
            to_west(part, g).wait_recv()
            to_east(part, g).wait_recv()
            slabs = [west_ref.at[part, g]]
            slabs += [own_ref.at[part, s, g] for s in range(SIDES)]
            slabs += [east_ref.at[part, g]]

            def advect(i, carry, part=part, slabs=slabs):
                def read(slab, column, block):
                    flat = slab.reshape(rows, LANES)
                    return [
                        flat[pl.ds(block * (8 * ROWS) + t * COLUMNS + column, 8, stride=ROWS), :]
                        for t in range(BLOCKS)
                    ]

                def shifts(values):
                    return south_of(values, lane), north_of(values, lane)

                blocks = [i * batch + j for j in range(batch)]
                cols = [
                    [read(slab, column, block) for slab in slabs for column in range(COLUMNS)]
                    for block in blocks
                ]
                moved = [[shifts(c[at + 1]) for at in range(width + 2)] for c in cols]
                mid = [
                    [step(c[at : at + 3], at, m[at]) for at in range(width + 2)]
                    for c, m in zip(cols, moved)
                ]
                moved = [[shifts(c[at + 1]) for at in range(width)] for c in mid]
                for block, c, m in zip(blocks, mid, moved):
                    for at in range(width):
                        new = step(c[at : at + 3], at + 1, m[at])
                        for t in range(BLOCKS):
                            place = at // COLUMNS * ROWS + t * COLUMNS + at % COLUMNS
                            begin = (part * count + block * 8) * PITCH + place
                            c_ref[pl.ds(begin, 8, stride=PITCH), :] = new[t]
                return carry

            lax.fori_loop(0, count // (8 * batch), advect, 0)

        @pl.when(g + 1 < groups)
        def _():
            pass_on(g + 1, range(parts - 1))

        def react(repeat, carry):
            def velocities(i, carry):
                for j in range(UNROLL):
                    r = i * UNROLL + j
                    one, two = first_at[r], second_at[r]
                    for at in (0, STRIP - 8):
                        w_ref[pl.ds(r * PITCH + at, 8), :] = (
                            c_ref[pl.ds(one + at, 8), :] * c_ref[pl.ds(two + at, 8), :]
                        )
                return carry

            lax.fori_loop(0, reactions // UNROLL, velocities, 0)

            for k in range(STRIP):
                w = w_ref[pl.ds(k, reactions, stride=PITCH), :] * k_ref[...]
                high = w.astype(jnp.bfloat16)
                low = (w - high.astype(jnp.float32)).astype(jnp.bfloat16)
                change = jnp.dot(
                    table_ref[...],
                    jnp.concatenate([high, low], axis=1),
                    preferred_element_type=jnp.float32,
                )
                where = pl.ds(k, species, stride=PITCH)
                c_ref[where, :] = c_ref[where, :] + (change[:, :LANES] + change[:, LANES:])

            @pl.when(jnp.logical_and(repeat == 0, g + 1 < groups))
            def _():
                pass_on(g + 1, range(parts - 1, parts))

            return carry

        lax.fori_loop(0, SUBSTEPS, react, 0)

        for part in range(parts):

            def put(i, carry, part=part):
                for s in range(SIDES):
                    flat = stage_ref.at[part, s, g].reshape(rows, LANES)
                    for k in range(ROWS):
                        begin = (part * count + i * 8) * PITCH + s * ROWS + k
                        flat[pl.ds(i * (8 * ROWS) + k, 8, stride=ROWS), :] = c_ref[
                            pl.ds(begin, 8, stride=PITCH), :
                        ]
                return carry

            lax.fori_loop(0, count // 8, put, 0)
        for pair in reversed(pairs):
            start(*give_back(*pair, g))
        return carry

    lax.fori_loop(0, groups, one_group, 0)

    def finish(g, carry):
        for pair in pairs:
            for _, there, maybe_here in (gather(*pair, g), give_back(*pair, g)):
                sent(there, maybe_here)
            returned(*pair, g).wait_recv()
        for part in range(parts):
            to_west(part, g).wait_send()
            to_east(part, g).wait_send()
        return carry

    lax.fori_loop(0, groups, finish, 0)


def body(tracers, fluxes, rate_coeff, first_reactant, second_reactant, product_species):
    parts = lax.axis_size("tracer")
    count, columns, length = tracers.shape
    total = length // GROUP
    groups = total // (2 * parts)
    species = parts * count
    reactions = rate_coeff.shape[0]

    def by_block(values):
        lead = values.shape[0]
        blocks = values.shape[2] // LANES
        return (
            values.reshape(lead, columns, blocks, LANES)
            .transpose(0, 2, 1, 3)
            .reshape(lead, blocks // BLOCKS, BLOCKS, columns, LANES)
        )

    natural = by_block(tracers)
    smem = pl.BlockSpec(memory_space=pltpu.SMEM)
    vmem = pl.BlockSpec(memory_space=pltpu.VMEM)
    anywhere = pl.BlockSpec(memory_space=pl.ANY)
    tile = (BLOCKS, columns, LANES)
    f32 = jnp.float32
    dma = pltpu.SemaphoreType.DMA
    coefs = (SIDES * columns + 2) * BLOCKS * 5
    out = pl.pallas_call(
        functools.partial(kernel, parts, count, groups),
        out_shape=jax.ShapeDtypeStruct(natural.shape, f32),
        in_specs=[smem] * 3 + [vmem] * 3 + [anywhere] * 2,
        out_specs=vmem,
        scratch_shapes=[pltpu.VMEM((parts, SIDES, groups, count, *tile), f32)] * 2
        + [pltpu.VMEM((parts, groups, count, *tile), f32)] * 2
        + [pltpu.VMEM((SIDES, 2, groups, *tile), f32)]
        + [pltpu.VMEM((2, groups, *tile), f32)] * 2
        + [
            pltpu.VMEM((coefs, -(-groups // 8) * 8, LANES), f32),
            pltpu.VMEM((coefs, 8, LANES), f32),
            pltpu.VMEM((species * PITCH + 8, LANES), f32),
            pltpu.VMEM((reactions * PITCH + 8, LANES), f32),
            pltpu.VMEM((reactions, LANES), f32),
            pltpu.VMEM((species, reactions), jnp.bfloat16),
            pltpu.SMEM((reactions,), jnp.int32),
            pltpu.SMEM((reactions,), jnp.int32),
        ]
        + [dma((parts, 2, groups))] * 4
        + [dma((parts, groups))] * 4
        + [dma((2,))] * 4,
        compiler_params=pltpu.CompilerParams(
            vmem_limit_bytes=45 * 1024 * 1024, collective_id=0, has_side_effects=True
        ),
        name="belt",
    )(
        *[
            pltpu.with_memory_space_constraint(x, pltpu.HBM)
            for x in (
                first_reactant,
                second_reactant,
                rate_coeff,
                first_reactant[None, :],
                second_reactant[None, :],
                product_species[None, :],
                by_block(fluxes),
                natural,
            )
        ]
    )
    return (
        out.reshape(count, total * BLOCKS, columns, LANES).transpose(0, 2, 1, 3).reshape(tracers.shape)
    )


def solution(mesh):
    in_specs = (P("tracer", "region", None), P(None, "region", "tracer"), P(), P(), P(), P())
    out_specs = P("tracer", "region", None)
    return jax.shard_map(body, mesh=mesh, in_specs=in_specs, out_specs=out_specs, check_vma=False)
```

```python
import functools

import jax
import jax.numpy as jnp
from jax import lax
from jax.experimental import pallas as pl
from jax.experimental.pallas import tpu as pltpu
from jax.sharding import PartitionSpec as P

NY = 48
SUBSTEPS = 4
LANES = 128
BLOCKS = 3
COLUMNS = 2
ROWS = COLUMNS * BLOCKS
GROUP = BLOCKS * LANES
SIDES = 2
STRIP = SIDES * ROWS
PITCH = STRIP + 1
UNROLL = 64
MESH = pl.DeviceIdType.MESH


def south_of(values, lane):
    shifted = []
    for t in range(BLOCKS):
        source = values[t] if t == 0 else jnp.where(lane == LANES - 1, values[t - 1], values[t])
        shifted.append(pltpu.roll(source, 1, 1))
    return shifted


def north_of(values, lane):
    shifted = []
    for t in range(BLOCKS):
        last = t == BLOCKS - 1
        source = values[t] if last else jnp.where(lane == 0, values[t + 1], values[t])
        shifted.append(pltpu.roll(source, LANES - 1, 1))
    return shifted


def up(values):
    return jnp.maximum(values, 0.0)


def down(values):
    return jnp.minimum(values, 0.0)


def write_coefficients(groups, coef_ref, own_ref, west_ref, east_ref):
    lane = lax.broadcasted_iota(jnp.int32, (groups, LANES), 1)

    def read(ref, axis, column):
        rows = ref.reshape(2 * groups * ROWS, LANES)
        return [
            rows[pl.ds(axis * groups * ROWS + t * COLUMNS + column, groups, stride=ROWS), :]
            for t in range(BLOCKS)
        ]

    sources = [(west_ref, COLUMNS - 1)]
    sources += [(own_ref.at[side], column) for side in range(SIDES) for column in range(COLUMNS)]
    sources += [(east_ref, 0), (east_ref, 1)]
    u = [read(ref, 0, column) for ref, column in sources]
    for at in range(len(sources) - 1):
        v = read(sources[at][0], 1, sources[at][1])
        above = north_of(v, lane)
        for t in range(BLOCKS):
            y = (lane + t * LANES) % NY
            bottom, top = y == 0, y == NY - 1
            west_face, east_face = u[at][t], u[at + 1][t]
            center = (
                1.0
                + down(west_face)
                - up(east_face)
                + jnp.where(bottom, 0.0, down(v[t]))
                - jnp.where(top, 0.0, up(above[t]))
            )
            south = jnp.where(bottom, 0.0, up(v[t]))
            north = jnp.where(top, 0.0, -down(above[t]))
            for m, value in enumerate((center, up(west_face), -down(east_face), south, north)):
                coef_ref[(at * BLOCKS + t) * 5 + m, pl.ds(0, groups), :] = value


def kernel(
    parts,
    count,
    groups,
    first_ref,
    second_ref,
    rate_ref,
    first_row,
    second_row,
    product_row,
    flux_ref,
    nat_ref,
    out_ref,
    own_ref,
    stage_ref,
    west_ref,
    east_ref,
    flux_own,
    flux_west,
    flux_east,
    coef_ref,
    now_ref,
    c_ref,
    w_ref,
    k_ref,
    table_ref,
    first_at,
    second_at,
    g_send,
    g_recv,
    r_send,
    r_recv,
    w_send,
    w_recv,
    e_send,
    e_recv,
    f_send,
    f_recv,
    fh_send,
    fh_recv,
):
    region, me = lax.axis_index("region"), lax.axis_index("tracer")
    strips = lax.axis_size("region") // SIDES
    quad, bit, side = region // 4, (region // 2) % 2, region % 2
    strip = quad * 2 + side
    home = side == bit
    reactions = first_ref.shape[0]
    species = parts * count
    rows = count * ROWS

    def seat(at, b):
        return (at // 2) * 4 + b * 2 + at % 2

    west, east = seat((strip + strips - 1) % strips, bit), seat((strip + 1) % strips, bit)
    outer = jnp.where(side == 0, west, east)

    barrier = pltpu.get_barrier_semaphore()
    for shift in range(parts):
        for d in range(2):
            for e in range(2):
                if shift or d or e:
                    pl.semaphore_signal(
                        barrier,
                        1,
                        device_id=(quad * 4 + (bit + d) % 2 * 2 + (side + e) % 2, (me + shift) % parts),
                        device_id_type=MESH,
                    )
    pl.semaphore_signal(barrier, 1, device_id=(outer, me), device_id_type=MESH)
    pl.semaphore_wait(barrier, 4 * parts)

    def remote(source, target, send, recv, device):
        return pltpu.make_async_remote_copy(
            src_ref=source,
            dst_ref=target,
            send_sem=send,
            recv_sem=recv,
            device_id=device,
            device_id_type=MESH,
        )

    def start(copy_here, copy_there, maybe_here):
        if maybe_here:

            @pl.when(home)
            def _():
                copy_here().start()

            @pl.when(jnp.logical_not(home))
            def _():
                copy_there().start()

        else:
            copy_there().start()

    def sent(copy_there, maybe_here):
        if maybe_here:

            @pl.when(jnp.logical_not(home))
            def _():
                copy_there().wait_send()

        else:
            copy_there().wait_send()

    def gather(shift, d, g):
        owner, half = (me + shift) % parts, (bit + d) % 2
        source = nat_ref.at[:, (owner * 2 + half) * groups + g]
        target, arrived = own_ref.at[me, side, g], g_recv.at[me, side, g]
        return (
            lambda: pltpu.make_async_copy(source, target, arrived),
            lambda: remote(source, target, g_send.at[shift, d, g], arrived, (seat(quad * 2 + bit, half), owner)),
            shift == 0 and d == 0,
        )

    def gathered(part, s, g):
        return remote(
            own_ref.at[part, s, g], own_ref.at[part, s, g], g_send.at[0, 0, g], g_recv.at[part, s, g], (east, me)
        )

    def to_west(part, g):
        return remote(
            own_ref.at[part, 0, g], east_ref.at[part, g], e_send.at[part, g], e_recv.at[part, g], (west, me)
        )

    def to_east(part, g):
        return remote(
            own_ref.at[part, 1, g], west_ref.at[part, g], w_send.at[part, g], w_recv.at[part, g], (east, me)
        )

    def give_back(shift, e, g):
        part, s = (me + parts - shift) % parts, (side + e) % 2
        source, target = stage_ref.at[part, s, g], out_ref.at[:, (me * 2 + bit) * groups + g]
        arrived = r_recv.at[shift, (bit + side) % 2, g]
        return (
            lambda: pltpu.make_async_copy(source, target, arrived),
            lambda: remote(source, target, r_send.at[shift, e, g], arrived, (quad * 4 + side * 2 + s, part)),
            shift == 0 and e == 0,
        )

    def returned(shift, d, g):
        target = out_ref.at[:, g]
        return remote(stage_ref.at[0, 0, g], target, r_send.at[0, 0, g], r_recv.at[shift, d, g], (east, me))

    pairs = [(shift, d) for shift in (*range(1, parts), 0) for d in (1, 0)]

    def flux_gather(d):
        half = (bit + d) % 2
        source = flux_ref.at[:, pl.ds(half * groups, groups)]
        target, arrived = flux_own.at[side], f_recv.at[side]
        return (
            lambda: pltpu.make_async_copy(source, target, arrived),
            lambda: remote(source, target, f_send.at[d], arrived, (seat(quad * 2 + bit, half), me)),
            d == 0,
        )

    def flux_gathered(s):
        return remote(flux_own.at[s], flux_own.at[s], f_send.at[0], f_recv.at[s], (east, me))

    def flux_halo():
        return (
            remote(flux_own.at[0], flux_east, fh_send.at[0], fh_recv.at[0], (west, me)),
            remote(flux_own.at[1], flux_west, fh_send.at[1], fh_recv.at[1], (east, me)),
        )

    def pass_on(g, shifts):
        for shift in shifts:
            part = (me + shift + jnp.where(home, 0, 1)) % parts
            for s, onward in ((0, to_west), (1, to_east)):
                gathered(part, s, g).wait_recv()
                onward(part, g).start()

    for d in (1, 0):
        start(*flux_gather(d))
    straight = [pair for pair in pairs if pair[0] and not pair[1]]
    far = [pair for pair in pairs if pair[0] and pair[1]]
    for g in range(groups):

        @pl.when(side == 0)
        def _(g=g):
            for pair in far + straight:
                start(*gather(*pair, g))

        @pl.when(side != 0)
        def _(g=g):
            for pair in straight + far:
                start(*gather(*pair, g))

        for pair in pairs:
            if pair not in far and pair not in straight:
                start(*gather(*pair, g))

    def prepare(r, carry):
        first_at[r] = first_ref[r] * PITCH
        second_at[r] = second_ref[r] * PITCH
        k_ref[pl.ds(r, 1), :] = jnp.full((1, LANES), rate_ref[r], jnp.float32)
        return carry

    lax.fori_loop(0, reactions, prepare, 0)

    def build(i, carry):
        at = pl.multiple_of(i * 16, 16)
        order = lax.broadcasted_iota(jnp.int32, (16, reactions), 0) + at
        table_ref[pl.ds(at, 16), :] = (
            (product_row[...] == order).astype(jnp.float32)
            - (first_row[...] == order).astype(jnp.float32)
            - (second_row[...] == order).astype(jnp.float32)
        ).astype(jnp.bfloat16)
        return carry

    lax.fori_loop(0, species // 16, build, 0)

    for s in range(SIDES):
        flux_gathered(s).wait_recv()
    for copy in flux_halo():
        copy.start()
    for copy in flux_halo():
        copy.wait()
    for d in (1, 0):
        _, there, maybe_here = flux_gather(d)
        sent(there, maybe_here)
    write_coefficients(groups, coef_ref, flux_own, flux_west, flux_east)
    pass_on(0, range(parts))

    lane = lax.broadcasted_iota(jnp.int32, (8, LANES), 1)
    batch = max(b for b in (1, 2, 4) if count % (8 * b) == 0)

    def one_group(g, carry):
        def spread(i, carry):
            now_ref[i, :, :] = coef_ref[i, pl.ds(g, 8, stride=0), :]
            return carry

        lax.fori_loop(0, coef_ref.shape[0], spread, 0)
        def step(cols, at, shifted):
            south, north = shifted
            return [
                now_ref[(at * BLOCKS + t) * 5, :, :] * cols[1][t]
                + now_ref[(at * BLOCKS + t) * 5 + 1, :, :] * cols[0][t]
                + now_ref[(at * BLOCKS + t) * 5 + 2, :, :] * cols[2][t]
                + now_ref[(at * BLOCKS + t) * 5 + 3, :, :] * south[t]
                + now_ref[(at * BLOCKS + t) * 5 + 4, :, :] * north[t]
                for t in range(BLOCKS)
            ]

        width = SIDES * COLUMNS
        for shift in range(parts):
            part = (me + shift + jnp.where(home, 0, 1)) % parts
            to_west(part, g).wait_recv()
            to_east(part, g).wait_recv()
            slabs = [west_ref.at[part, g]]
            slabs += [own_ref.at[part, s, g] for s in range(SIDES)]
            slabs += [east_ref.at[part, g]]

            def advect(i, carry, part=part, slabs=slabs):
                def read(slab, column, block):
                    flat = slab.reshape(rows, LANES)
                    return [
                        flat[pl.ds(block * (8 * ROWS) + t * COLUMNS + column, 8, stride=ROWS), :]
                        for t in range(BLOCKS)
                    ]

                def shifts(values):
                    return south_of(values, lane), north_of(values, lane)

                blocks = [i * batch + j for j in range(batch)]
                cols = [
                    [read(slab, column, block) for slab in slabs for column in range(COLUMNS)]
                    for block in blocks
                ]
                moved = [[shifts(c[at + 1]) for at in range(width + 2)] for c in cols]
                mid = [
                    [step(c[at : at + 3], at, m[at]) for at in range(width + 2)]
                    for c, m in zip(cols, moved)
                ]
                moved = [[shifts(c[at + 1]) for at in range(width)] for c in mid]
                for block, c, m in zip(blocks, mid, moved):
                    for at in range(width):
                        new = step(c[at : at + 3], at + 1, m[at])
                        for t in range(BLOCKS):
                            place = at // COLUMNS * ROWS + t * COLUMNS + at % COLUMNS
                            begin = (part * count + block * 8) * PITCH + place
                            c_ref[pl.ds(begin, 8, stride=PITCH), :] = new[t]
                return carry

            lax.fori_loop(0, count // (8 * batch), advect, 0)

        @pl.when(g + 1 < groups)
        def _():
            pass_on(g + 1, range(parts - 1))

        def react(repeat, carry):
            def velocities(i, carry):
                for j in range(UNROLL):
                    r = i * UNROLL + j
                    one, two = first_at[r], second_at[r]
                    for at in (0, STRIP - 8):
                        w_ref[pl.ds(r * PITCH + at, 8), :] = (
                            c_ref[pl.ds(one + at, 8), :] * c_ref[pl.ds(two + at, 8), :]
                        )
                return carry

            lax.fori_loop(0, reactions // UNROLL, velocities, 0)

            for k in range(STRIP):
                w = w_ref[pl.ds(k, reactions, stride=PITCH), :] * k_ref[...]
                high = w.astype(jnp.bfloat16)
                low = (w - high.astype(jnp.float32)).astype(jnp.bfloat16)
                change = jnp.dot(
                    table_ref[...],
                    jnp.concatenate([high, low], axis=1),
                    preferred_element_type=jnp.float32,
                )
                where = pl.ds(k, species, stride=PITCH)
                c_ref[where, :] = c_ref[where, :] + (change[:, :LANES] + change[:, LANES:])

            @pl.when(jnp.logical_and(repeat == 0, g + 1 < groups))
            def _():
                pass_on(g + 1, range(parts - 1, parts))

            return carry

        lax.fori_loop(0, SUBSTEPS, react, 0)

        for part in range(parts):

            def put(i, carry, part=part):
                for s in range(SIDES):
                    flat = stage_ref.at[part, s, g].reshape(rows, LANES)
                    for k in range(ROWS):
                        begin = (part * count + i * 8) * PITCH + s * ROWS + k
                        flat[pl.ds(i * (8 * ROWS) + k, 8, stride=ROWS), :] = c_ref[
                            pl.ds(begin, 8, stride=PITCH), :
                        ]
                return carry

            lax.fori_loop(0, count // 8, put, 0)
        for pair in reversed(pairs):
            start(*give_back(*pair, g))
        return carry

    lax.fori_loop(0, groups, one_group, 0)

    def finish(g, carry):
        for pair in pairs:
            for _, there, maybe_here in (gather(*pair, g), give_back(*pair, g)):
                sent(there, maybe_here)
            returned(*pair, g).wait_recv()
        for part in range(parts):
            to_west(part, g).wait_send()
            to_east(part, g).wait_send()
        return carry

    lax.fori_loop(0, groups, finish, 0)


def body(tracers, fluxes, rate_coeff, first_reactant, second_reactant, product_species):
    parts = lax.axis_size("tracer")
    count, columns, length = tracers.shape
    total = length // GROUP
    groups = total // (2 * parts)
    species = parts * count
    reactions = rate_coeff.shape[0]

    def by_block(values):
        lead = values.shape[0]
        blocks = values.shape[2] // LANES
        return (
            values.reshape(lead, columns, blocks, LANES)
            .transpose(0, 2, 1, 3)
            .reshape(lead, blocks // BLOCKS, BLOCKS, columns, LANES)
        )

    natural = by_block(tracers)
    smem = pl.BlockSpec(memory_space=pltpu.SMEM)
    vmem = pl.BlockSpec(memory_space=pltpu.VMEM)
    anywhere = pl.BlockSpec(memory_space=pl.ANY)
    tile = (BLOCKS, columns, LANES)
    f32 = jnp.float32
    dma = pltpu.SemaphoreType.DMA
    coefs = (SIDES * columns + 2) * BLOCKS * 5
    out = pl.pallas_call(
        functools.partial(kernel, parts, count, groups),
        out_shape=jax.ShapeDtypeStruct(natural.shape, f32),
        in_specs=[smem] * 3 + [vmem] * 3 + [anywhere] * 2,
        out_specs=vmem,
        scratch_shapes=[pltpu.VMEM((parts, SIDES, groups, count, *tile), f32)] * 2
        + [pltpu.VMEM((parts, groups, count, *tile), f32)] * 2
        + [pltpu.VMEM((SIDES, 2, groups, *tile), f32)]
        + [pltpu.VMEM((2, groups, *tile), f32)] * 2
        + [
            pltpu.VMEM((coefs, -(-groups // 8) * 8, LANES), f32),
            pltpu.VMEM((coefs, 8, LANES), f32),
            pltpu.VMEM((species * PITCH + 8, LANES), f32),
            pltpu.VMEM((reactions * PITCH + 8, LANES), f32),
            pltpu.VMEM((reactions, LANES), f32),
            pltpu.VMEM((species, reactions), jnp.bfloat16),
            pltpu.SMEM((reactions,), jnp.int32),
            pltpu.SMEM((reactions,), jnp.int32),
        ]
        + [dma((parts, 2, groups))] * 4
        + [dma((parts, groups))] * 4
        + [dma((2,))] * 4,
        compiler_params=pltpu.CompilerParams(
            vmem_limit_bytes=45 * 1024 * 1024, collective_id=0, has_side_effects=True
        ),
        name="belt",
    )(
        *[
            pltpu.with_memory_space_constraint(x, pltpu.HBM)
            for x in (
                first_reactant,
                second_reactant,
                rate_coeff,
                first_reactant[None, :],
                second_reactant[None, :],
                product_species[None, :],
                by_block(fluxes),
                natural,
            )
        ]
    )
    return (
        out.reshape(count, total * BLOCKS, columns, LANES).transpose(0, 2, 1, 3).reshape(tracers.shape)
    )


def solution(mesh):
    in_specs = (P("tracer", "region", None), P(None, "region", "tracer"), P(), P(), P(), P())
    out_specs = P("tracer", "region", None)
    return jax.shard_map(body, mesh=mesh, in_specs=in_specs, out_specs=out_specs, check_vma=False)
```
